128 devices in a mesh: spec: 8 (over y, core), mass: 16 (over z, x).
Axes of the slice: x: 4, y: 4, z: 4, core: 2. Of those that a mesh axis runs over, the one named last changes fastest.
Arguments:
- spectra: bfloat16 [4096, 2048], P(('spec', 'mass')), may hold values from 0.001 to 10000, as said below
- routes: int32 [4096, 2], P(('spec', 'mass')), may hold values from 0 to 47, all different within a row; in each aligned block of 32 rows (0 to 31, 32 to 63, ...) at most 2 rows name the same one
- pep_bins: int32 [48, 32, 4096], P('mass', None, 'spec'), may hold values from 0 to 2047
- counts: int32 [48], replicated, may hold values from 2048 to 4096
Outputs:
- xcorr_best: float32 [4096, 2], P(('spec', 'mass'))
- xcorr_z: float32 [4096, 2], P(('spec', 'mass'))
The draws below stay inside these ranges and needn't reach their ends.
Inputs may be any that keep to these rules, and one draw needn't show every extreme that they name: `routes`: among the rows of one device each window is named by at most 2 entries, and in some device by exactly 2. `spectra`: intensities are positive.
All inputs are finite; a program needn't handle non-finite values.
Results may differ from the reference program's by a relative error of at most 0.005.
Values may be sent and summed in bfloat16 or wider, within the bound.
No kernel may reach another device: no remote copies, remote signals or barrier semaphores. Data moves between devices by JAX's collectives and lax.ppermute only.
A program may use at most 64 MiB of HBM per device.

```python
import math
import jax
import jax.numpy as jnp
import numpy as np
from jax import lax

BINS = 2048
PEPS = 4096
FRAG = 32
LAG = 75
TOPW = 2
SPEC_DEV = 32
SPECTRA = 4096
WINDOWS = 48
CAP = 2
N_SPEC = 8
N_MASS = 16


def draw_spectra(key, part):
    first_key, second_key = jax.random.split(key)
    levels = jax.random.uniform(first_key, (SPECTRA, BINS), jnp.float32, math.log(0.01), math.log(100.0))
    scales = jax.random.uniform(second_key, (SPECTRA, 1), jnp.float32, 0.0, math.log(100.0))
    return (jnp.exp(levels) * jnp.exp(scales)).astype(jnp.bfloat16)


def touch_ends(array, key, least, top_value):
    shape = array.shape
    index_at = [jax.random.randint(jax.random.fold_in(key, axis), (), 0, shape[axis]) for axis in range(len(shape))]
    array = array.at[tuple(index_at)].set(least)
    longest = shape.index(max(shape))
    index_at[longest] = (index_at[longest] + 1) % shape[longest]
    return array.at[tuple(index_at)].set(top_value)


def deal_out(rng, own, number, rows, number_of, top, most, skew):
    sequence = jax.random.permutation(rng, number_of)
    crowded, ordinary = shares(number_of, rows * top, most, skew, True), shares(number_of, rows * top, most, skew, False)
    places = jnp.arange(number_of)

    def named(tallies, rotation):
        used = int((tallies > 0).sum())
        fixed = max(1, used // 4)
        passed = fixed + (places - fixed + rotation * (used - fixed)) % max(1, number_of - fixed)
        return jnp.zeros((number_of,), jnp.int32).at[sequence[jnp.where(places < fixed, places, passed)]].set(jnp.asarray(tallies, jnp.int32))

    tallies = jnp.where(number % 4 == 0, named(crowded, number // 4), named(ordinary, number - number // 4 - 1))
    mixed = jax.random.permutation(jax.random.fold_in(own, 3), number_of)
    giver, taker = mixed[0:number_of // 2 * 2:2], mixed[1:number_of // 2 * 2:2]
    room = jnp.minimum(tallies[giver] - 1, most - tallies[taker]) // 2
    room = jnp.where((giver == sequence[0]) | (taker == sequence[0]) | (tallies[taker] == 0), 0, jnp.maximum(room, 0))
    passed = jax.random.randint(jax.random.fold_in(own, 4), (number_of // 2,), 0, 1 << 20) % (room + 1)
    tallies = tallies.at[giver].add(-passed).at[taker].add(passed)
    labels = jnp.searchsorted(jnp.cumsum(tallies), jnp.arange(rows * top), side="right").astype(jnp.int32)
    grid = labels.reshape(top, rows).T
    grid = grid[jax.random.permutation(jax.random.fold_in(own, 1), rows)]
    rotation = jax.random.randint(jax.random.fold_in(own, 2), (rows, 1), 0, top)
    return jnp.take_along_axis(grid, (jnp.arange(top)[None, :] + rotation) % top, axis=1)


def shares(number_of, total, most, lean, full):
    portions = [(1 << 20) // math.isqrt(rank ** lean) + 1 for rank in range(1, number_of + 1)]
    largest = most if full else min(most, max(-(-total // number_of), total * portions[0] // sum(portions)))
    least = 1 if total - largest >= number_of - 1 else 0
    given, rest = [largest] + [least] * (number_of - 1), total - largest - least * (number_of - 1)
    while rest > 0:
        candidates = [i for i in range(1, number_of) if given[i] < largest] or [i for i in range(1, number_of) if given[i] < most]
        pool, remaining = sum([portions[i] for i in candidates]), rest
        for i in candidates:
            extra = min(most - given[i], max(1, remaining * portions[i] // pool), rest)
            given[i] = given[i] + extra
            rest = rest - extra
    return np.array(given)


def setup_inputs(seed: int = 0) -> dict:
    streams_of = jax.random.split(jax.random.key(seed), 5)
    spectra = draw_spectra(jax.random.fold_in(streams_of[4], 71), 0)
    routes_keys = jax.random.split(jax.random.fold_in(streams_of[1], 1), SPECTRA // SPEC_DEV)
    routes_turns = jax.random.permutation(jax.random.fold_in(streams_of[1], 3), SPECTRA // SPEC_DEV)
    routes = jax.vmap(lambda own, number: deal_out(jax.random.fold_in(streams_of[1], 2), own, number, SPEC_DEV, WINDOWS, TOPW, CAP, 1))(routes_keys, routes_turns).reshape((SPECTRA, TOPW))
    pep_bins = touch_ends(jax.random.randint(streams_of[2], (WINDOWS, FRAG, PEPS), 0, BINS), jax.random.fold_in(streams_of[2], 1), 0, BINS - 1).astype(jnp.int32)
    counts = touch_ends(jax.random.randint(streams_of[3], (WINDOWS,), PEPS // 2, PEPS + 1), jax.random.fold_in(streams_of[3], 1), PEPS // 2, PEPS).astype(jnp.int32)
    return dict(spectra=spectra, routes=routes, pep_bins=pep_bins, counts=counts)


EPS = 1e-06

def band_matrix(width, dtype):
    offset = jnp.abs(jnp.arange(width)[:, None] - jnp.arange(width)[None, :])
    return ((offset <= LAG) & (offset > 0)).astype(dtype)

def reference(spectra, routes, pep_bins, counts):
    band_rows = band_matrix(BINS, jnp.float32)
    rooted = jnp.sqrt(spectra.astype(jnp.float32)).astype(jnp.bfloat16)

    def prepare_block(block):
        values = block.astype(jnp.float32)
        background = jnp.dot(values, band_rows, precision=lax.Precision.HIGHEST)
        return (values - background / (2.0 * LAG)).astype(jnp.bfloat16)
    prepared = lax.map(prepare_block, rooted.reshape(-1, SPEC_DEV, BINS)).reshape(SPECTRA, BINS)
    flat_windows = routes.reshape(-1)
    entries = flat_windows.shape[0]
    source_rows = (jnp.arange(entries) // TOPW).astype(jnp.int32)
    limit = N_SPEC * N_MASS * CAP
    pep_index = jnp.arange(PEPS)

    def one_window(carry, window_id):
        out_best, out_z = carry
        hit = flat_windows == window_id
        position = jnp.cumsum(hit.astype(jnp.int32)) - 1
        position = jnp.where(hit, position, limit).astype(jnp.int32)
        picked = jnp.zeros((limit + 1,), jnp.int32).at[position].set(source_rows)
        rows_now = prepared[picked[:limit]].astype(jnp.float32)
        theory = jnp.zeros((BINS, PEPS), jnp.float32).at[pep_bins[window_id], pep_index[None, :]].add(1.0)
        scores = jnp.dot(rows_now, theory, precision=lax.Precision.HIGHEST) / FRAG
        valid = (pep_index < counts[window_id])[None, :]
        highest = lax.optimization_barrier(jnp.max(jnp.where(valid, scores, -1e+30), axis=1))
        total = lax.optimization_barrier(jnp.sum(jnp.where(valid, scores, 0.0), axis=1))
        square = lax.optimization_barrier(jnp.sum(jnp.where(valid, scores * scores, 0.0), axis=1))
        live_count = counts[window_id].astype(jnp.float32)
        mean_score = total / live_count
        spread = square / live_count - mean_score * mean_score
        standard = (highest - mean_score) / jnp.sqrt(spread + EPS)
        index_now = jnp.minimum(position, limit - 1)
        out_best = jnp.where(hit, highest[index_now], out_best)
        out_z = jnp.where(hit, standard[index_now], out_z)
        return ((out_best, out_z), None)
    start = (jnp.zeros((entries,), jnp.float32), jnp.zeros((entries,), jnp.float32))
    (out_best, out_z), unused = lax.scan(one_window, start, jnp.arange(WINDOWS).astype(jnp.int32))
    return (out_best.reshape(SPECTRA, TOPW), out_z.reshape(SPECTRA, TOPW))
```

```python
import functools

import jax
import jax.numpy as jnp
from jax import lax
from jax.experimental import pallas as pl
from jax.experimental.pallas import tpu as pltpu
from jax.sharding import PartitionSpec as P

LAG = 75
EPS = 1e-06
PAD = 128
SLOTS = 8
LOW = 128
HIGH = 16
F8 = jnp.float8_e4m3fn
VMEM = pltpu.VMEM
SMEM = pltpu.SMEM


def iota(shape, axis):
    return lax.broadcasted_iota(jnp.int32, shape, axis)


def prepare_kernel(spectra_ref, routes_ref, pep_ref, out_ref, flat_ref, padded, turned):
    rows, width = spectra_ref.shape
    rooted = jnp.sqrt(spectra_ref[...].astype(jnp.float32)).astype(jnp.bfloat16)
    padded[:, :PAD] = jnp.zeros((rows, PAD), jnp.bfloat16)
    padded[:, PAD + width :] = jnp.zeros((rows, PAD), jnp.bfloat16)
    padded[:, PAD : PAD + width] = rooted
    block = 256
    gap = jnp.abs(iota((block + 2 * PAD, block), 0) - PAD - iota((block + 2 * PAD, block), 1))
    band = jnp.where((gap > 0) & (gap <= LAG), 1.0, 0.0).astype(jnp.bfloat16)
    total = out_ref.shape[0]
    place = iota((total, rows), 0)
    inner = place % SLOTS
    window = (place // SLOTS) * 3 + inner // 2
    named = (routes_ref[0:1, :] == window) | (routes_ref[1:2, :] == window)
    named = named & (inner < 6)
    before = jnp.where(iota((rows, rows), 0) < iota((rows, rows), 1), 1.0, 0.0)
    earlier = jnp.dot(
        jnp.where(named, 1.0, 0.0).astype(jnp.bfloat16),
        before.astype(jnp.bfloat16),
        preferred_element_type=jnp.float32,
    )
    taken = named & (earlier == (inner % 2).astype(jnp.float32))
    routing = jnp.where(taken, 1.0, 0.0).astype(jnp.bfloat16)
    for start in range(0, width, block):
        background = jnp.dot(
            padded[:, start : start + block + 2 * PAD], band, preferred_element_type=jnp.float32
        )
        values = rooted[:, start : start + block].astype(jnp.float32)
        prepared = (values - background / (2.0 * LAG)).astype(jnp.bfloat16)
        out_ref[:, start : start + block] = jnp.dot(
            routing, prepared, preferred_element_type=jnp.float32
        ).astype(jnp.bfloat16)
    lane = iota((128, 128), 1) // 32
    for step in range(pep_ref.shape[0]):
        table = pep_ref[step]
        turned[...] = jnp.concatenate([table] * 4, axis=0).T
        flat = jnp.zeros((128, 128), jnp.int32)
        for part in range(4):
            flat = jnp.where(lane == part, turned[pl.ds(part, 128, stride=4), :], flat)
        flat_ref[step] = flat.astype(jnp.int16)


def theory_kernel(flat_ref, theory_ref):
    width = flat_ref.shape[2]
    high_place = iota((HIGH * 8, 2 * width), 0).astype(jnp.float32).astype(jnp.bfloat16)
    low_place = iota((LOW, 2 * width), 0).astype(jnp.float32).astype(jnp.bfloat16)
    one = jnp.ones((), F8)
    zero = jnp.zeros((), F8)
    member = iota((128, 128), 1) // 32 + 4 * (iota((128, 128), 0) % 2)

    def window(step, carry):
        bins = flat_ref[step].astype(jnp.int32)
        low = (bins & (LOW - 1)).astype(jnp.float32).astype(jnp.bfloat16)
        high = ((bins >> 7) * 8 + member).astype(jnp.float32).astype(jnp.bfloat16)
        for pair in range(32):
            parts = []
            for half in range(2):
                row = 4 * pair + 2 * half
                high_row = jnp.concatenate([high[row : row + 1], high[row + 1 : row + 2]], axis=1)
                low_row = jnp.concatenate([low[row : row + 1], low[row + 1 : row + 2]], axis=1)
                parts.append(
                    lax.dot_general(
                        jnp.where(high_place == high_row, one, zero),
                        jnp.where(low_place == low_row, one, zero),
                        (((1,), (1,)), ((), ())),
                        preferred_element_type=jnp.float32,
                    )
                )
            for part in range(HIGH):
                tile = jnp.concatenate([item[part * 8 : part * 8 + 8] for item in parts], axis=0)
                theory_ref[step, pair * 16 : pair * 16 + 16, part * LOW : (part + 1) * LOW] = (
                    tile.astype(jnp.bfloat16)
                )
        return carry

    lax.fori_loop(0, flat_ref.shape[0], window, 0)


def build_theory(flat, width):
    steps = flat.shape[0]
    return pl.pallas_call(
        theory_kernel,
        out_shape=jax.ShapeDtypeStruct((steps, 512, width), jnp.bfloat16),
        in_specs=[pl.BlockSpec(memory_space=VMEM)],
        out_specs=pl.BlockSpec(memory_space=VMEM),
        compiler_params=pltpu.CompilerParams(vmem_limit_bytes=16 << 20),
        cost_estimate=pl.CostEstimate(
            flops=3_000_000_000, bytes_accessed=6_400_000, transcendentals=0
        ),
        name="theory",
    )(flat)


def score_kernel(counts_ref, t0, t1, t2, t3, own_ref, other_ref, out_ref):
    y = lax.axis_index("spec") // 2
    core = lax.axis_index("spec") % 2
    mass = lax.axis_index("mass")
    steps = t0.shape[0]
    rows = own_ref.shape[0] * 2
    spectra = jnp.concatenate([own_ref[...], other_ref[...]], axis=0)
    slot = (iota((1, rows), 1) % SLOTS) // 2
    local = iota((512, 1), 0)
    best = jnp.zeros((1, rows), jnp.float32)
    total = jnp.zeros((1, rows), jnp.float32)
    square = jnp.zeros((1, rows), jnp.float32)
    for step in range(steps):
        live = counts_ref[mass * steps + step]
        now_best, now_total, now_square = [], [], []
        for turn, theory in enumerate((t0, t1, t2, t3)):
            base = (((y + turn) % 4) * 2 + core) * 512
            scores = lax.dot_general(
                theory[step],
                spectra,
                (((1,), (1,)), ((), ())),
                preferred_element_type=jnp.float32,
            )
            valid = local < (live - base)
            now_best.append(
                jnp.max(jnp.where(valid, scores, -1e30), axis=0, keepdims=True)
            )
            scores = jnp.where(valid, scores, 0.0)
            now_total.append(jnp.sum(scores, axis=0, keepdims=True))
            now_square.append(jnp.sum(scores * scores, axis=0, keepdims=True))
        here = slot == step
        best = jnp.where(here, functools.reduce(jnp.maximum, now_best), best)
        total = jnp.where(here, sum(now_total[1:], now_total[0]), total)
        square = jnp.where(here, sum(now_square[1:], now_square[0]), square)
    stats = jnp.concatenate(
        [best / 32.0, total / 32.0, square / 1024.0, jnp.zeros((5, rows), jnp.float32)], axis=0
    )
    own, other = stats[:, : rows // 2], stats[:, rows // 2 :]
    first = jnp.where(core == 0, own, other)
    second = jnp.where(core == 0, other, own)
    peers = out_ref.shape[0] // 16
    for peer in range(peers):
        out_ref[peer * 8 : peer * 8 + 8, :] = first
        out_ref[(peers + peer) * 8 : (peers + peer) * 8 + 8, :] = second


def finish_kernel(counts_ref, routes_ref, stats_ref, best_ref, z_ref):
    rows = routes_ref.shape[1]
    mass = lax.axis_index("mass")
    windows = counts_ref.shape[1]
    picks = [routes_ref[0:1, :], routes_ref[1:2, :]]
    flat = jnp.concatenate(picks, axis=1)
    named_by = iota((windows, rows), 0)
    named = (picks[0] == named_by) | (picks[1] == named_by)
    before = jnp.where(iota((rows, rows), 0) < iota((rows, rows), 1), 1.0, 0.0)
    earlier = jnp.dot(
        jnp.where(named, 1.0, 0.0).astype(jnp.bfloat16),
        before.astype(jnp.bfloat16),
        preferred_element_type=jnp.float32,
    )
    slot = jnp.concatenate(
        [
            jnp.sum(jnp.where(pick == named_by, earlier, 0.0), axis=0, keepdims=True)
            for pick in picks
        ],
        axis=1,
    ).astype(jnp.int32)
    shard = flat // 3
    wanted = mass * SLOTS + (flat - shard * 3) * 2 + slot
    entries = 2 * rows
    lanes = stats_ref.shape[1]
    pick_lane = jnp.where(iota((lanes, entries), 0) == wanted, 1.0, 0.0)
    found = lax.dot_general(
        stats_ref[...],
        pick_lane,
        (((1,), (0,)), ((), ())),
        precision=lax.Precision.HIGHEST,
        preferred_element_type=jnp.float32,
    )
    peers = stats_ref.shape[0] // 16
    halves = []
    for half in range(2):
        chosen = jnp.zeros((8, entries), jnp.float32)
        for peer in range(peers):
            at = (half * peers + peer) * 8
            chosen = jnp.where(shard == peer, found[at : at + 8, :], chosen)
        halves.append(chosen)
    best = jnp.maximum(halves[0][0:1], halves[1][0:1])
    total = halves[0][1:2] + halves[1][1:2]
    square = halves[0][2:3] + halves[1][2:3]
    column = counts_ref[...].astype(jnp.float32)
    here = iota((entries, windows), 1)
    live = jnp.zeros((1, entries), jnp.float32)
    del here
    live = lax.dot_general(
        column,
        jnp.where(iota((windows, entries), 0) == flat, 1.0, 0.0),
        (((1,), (0,)), ((), ())),
        precision=lax.Precision.HIGHEST,
        preferred_element_type=jnp.float32,
    )
    mean = total / live
    spread = square / live - mean * mean
    z = (best - mean) / jnp.sqrt(spread + EPS)
    best_ref[0:1, :] = best[:, :rows]
    best_ref[1:2, :] = best[:, rows:]
    z_ref[0:1, :] = z[:, :rows]
    z_ref[1:2, :] = z[:, rows:]


def per_device(spectra, routes, pep_bins, counts):
    rows, width = spectra.shape
    mass_count = lax.axis_size("mass")
    spec_count = lax.axis_size("spec")
    steps = pep_bins.shape[0]
    routes_t = routes.T
    vmem = pl.BlockSpec(memory_space=VMEM)
    smem = pl.BlockSpec(memory_space=SMEM)
    outgoing, flat = pl.pallas_call(
        prepare_kernel,
        out_shape=(
            jax.ShapeDtypeStruct((mass_count * SLOTS, width), jnp.bfloat16),
            jax.ShapeDtypeStruct((steps, 128, 128), jnp.int16),
        ),
        in_specs=[vmem] * 3,
        out_specs=(vmem, vmem),
        scratch_shapes=[
            pltpu.VMEM((rows, width + 2 * PAD), jnp.bfloat16),
            pltpu.VMEM((512, 128), jnp.int32),
        ],
        compiler_params=pltpu.CompilerParams(vmem_limit_bytes=16 << 20),
        name="prepare",
    )(spectra, routes_t, pep_bins)
    flats = [flat] + [
        lax.ppermute(
            flat, "spec", [((i + 2 * turn) % spec_count, i) for i in range(spec_count)]
        )
        for turn in range(1, 4)
    ]
    own = lax.all_to_all(outgoing, "mass", split_axis=0, concat_axis=0, tiled=True)
    other = lax.ppermute(own, "spec", [(i, i ^ 1) for i in range(spec_count)])
    theories = [build_theory(item, width) for item in flats]
    stats = pl.pallas_call(
        score_kernel,
        out_shape=jax.ShapeDtypeStruct((2 * mass_count * 8, 128), jnp.float32),
        in_specs=[smem] + [vmem] * 6,
        out_specs=vmem,
        compiler_params=pltpu.CompilerParams(vmem_limit_bytes=48 << 20),
        name="score",
    )(counts, *theories, own, other)
    groups = [
        [(y * 2 + core) * mass_count + m for core in range(2) for m in range(mass_count)]
        for y in range(spec_count // 2)
    ]
    back = lax.all_to_all(
        stats,
        ("spec", "mass"),
        split_axis=0,
        concat_axis=0,
        tiled=True,
        axis_index_groups=groups,
    )
    best, z = pl.pallas_call(
        finish_kernel,
        out_shape=(jax.ShapeDtypeStruct((2, rows), jnp.float32),) * 2,
        in_specs=[vmem] * 3,
        out_specs=(vmem, vmem),
        name="finish",
    )(counts.reshape(1, -1), routes_t, back)
    return best.T, z.T


def solution(mesh):
    return jax.shard_map(
        per_device,
        mesh=mesh,
        in_specs=(
            P(("spec", "mass"), None),
            P(("spec", "mass"), None),
            P("mass", None, "spec"),
            P(),
        ),
        out_specs=(P(("spec", "mass"), None), P(("spec", "mass"), None)),
        check_vma=False,
    )
```

```python
import functools

import jax
import jax.numpy as jnp
from jax import lax
from jax.experimental import pallas as pl
from jax.experimental.pallas import tpu as pltpu
from jax.sharding import PartitionSpec as P

LAG = 75
EPS = 1e-06
PAD = 128
SLOTS = 8
LOW = 128
HIGH = 16
BUILT = 2
F8 = jnp.float8_e4m3fn
VMEM = pltpu.VMEM
SMEM = pltpu.SMEM


def iota(shape, axis):
    return lax.broadcasted_iota(jnp.int32, shape, axis)


def prepare_kernel(
    spectra_hbm,
    routes_hbm,
    pep_hbm,
    out_ref,
    flat_ref,
    spectra_ref,
    routes_ref,
    pep_ref,
    padded,
    turned,
    sems,
):
    copies = [
        pltpu.make_async_copy(spectra_hbm, spectra_ref, sems.at[0]),
        pltpu.make_async_copy(routes_hbm, routes_ref, sems.at[1]),
        pltpu.make_async_copy(pep_hbm, pep_ref, sems.at[2]),
    ]
    for copy in copies:
        copy.start()
    rows, width = spectra_ref.shape
    block = 256
    gap = jnp.abs(iota((block + 2 * PAD, block), 0) - PAD - iota((block + 2 * PAD, block), 1))
    band = jnp.where((gap > 0) & (gap <= LAG), 1.0, 0.0).astype(jnp.bfloat16)
    copies[0].wait()
    rooted = jnp.sqrt(spectra_ref[...].astype(jnp.float32)).astype(jnp.bfloat16)
    padded[:, :PAD] = jnp.zeros((rows, PAD), jnp.bfloat16)
    padded[:, PAD + width :] = jnp.zeros((rows, PAD), jnp.bfloat16)
    padded[:, PAD : PAD + width] = rooted
    copies[1].wait()
    total = out_ref.shape[0]
    place = iota((total, rows), 0)
    inner = place % SLOTS
    window = (place // SLOTS) * 3 + inner // 2
    named = (routes_ref[0:1, :] == window) | (routes_ref[1:2, :] == window)
    named = named & (inner < 6)
    before = jnp.where(iota((rows, rows), 0) < iota((rows, rows), 1), 1.0, 0.0)
    earlier = jnp.dot(
        jnp.where(named, 1.0, 0.0).astype(jnp.bfloat16),
        before.astype(jnp.bfloat16),
        preferred_element_type=jnp.float32,
    )
    taken = named & (earlier == (inner % 2).astype(jnp.float32))
    routing = jnp.where(taken, 1.0, 0.0).astype(jnp.bfloat16)
    for start in range(0, width, block):
        background = jnp.dot(
            padded[:, start : start + block + 2 * PAD], band, preferred_element_type=jnp.float32
        )
        values = rooted[:, start : start + block].astype(jnp.float32)
        prepared = (values - background / (2.0 * LAG)).astype(jnp.bfloat16)
        out_ref[:, start : start + block] = jnp.dot(
            routing, prepared, preferred_element_type=jnp.float32
        ).astype(jnp.bfloat16)
    copies[2].wait()
    lane = iota((128, 128), 1) // 32
    for step in range(pep_ref.shape[0]):
        table = pep_ref[step]
        turned[...] = jnp.concatenate([table] * 4, axis=0).T
        flat = jnp.zeros((128, 128), jnp.int32)
        for part in range(4):
            flat = jnp.where(lane == part, turned[pl.ds(part, 128, stride=4), :], flat)
        flat_ref[step] = flat.astype(jnp.int16)


def theory_of(bins, theory_ref):
    width = bins.shape[1]
    high_place = iota((HIGH * 8, 2 * width), 0).astype(jnp.float32).astype(jnp.bfloat16)
    low_place = iota((LOW, 2 * width), 0).astype(jnp.float32).astype(jnp.bfloat16)
    one = jnp.ones((), F8)
    zero = jnp.zeros((), F8)
    member = iota((128, 128), 1) // 32 + 4 * (iota((128, 128), 0) % 2)
    low = (bins & (LOW - 1)).astype(jnp.float32).astype(jnp.bfloat16)
    high = ((bins >> 7) * 8 + member).astype(jnp.float32).astype(jnp.bfloat16)
    for pair in range(32):
        parts = []
        for half in range(2):
            row = 4 * pair + 2 * half
            high_row = jnp.concatenate([high[row : row + 1], high[row + 1 : row + 2]], axis=1)
            low_row = jnp.concatenate([low[row : row + 1], low[row + 1 : row + 2]], axis=1)
            parts.append(
                lax.dot_general(
                    jnp.where(high_place == high_row, one, zero),
                    jnp.where(low_place == low_row, one, zero),
                    (((1,), (1,)), ((), ())),
                    preferred_element_type=jnp.float32,
                )
            )
        for part in range(HIGH):
            tile = jnp.concatenate([item[part * 8 : part * 8 + 8] for item in parts], axis=0)
            theory_ref[pair * 16 : pair * 16 + 16, part * LOW : (part + 1) * LOW] = tile.astype(
                jnp.bfloat16
            )


def theory_kernel(flat_ref, theory_ref, held, sems):
    steps = flat_ref.shape[0]

    def copy_of(step):
        return pltpu.make_async_copy(held.at[step], theory_ref.at[step], sems.at[step])

    def window(step, carry):
        theory_of(flat_ref[step].astype(jnp.int32), held.at[step])
        copy_of(step).start()
        return carry

    lax.fori_loop(0, steps, window, 0)
    for step in range(steps):
        copy_of(step).wait()


def build_theory(flat, width):
    steps = flat.shape[0]
    return pl.pallas_call(
        theory_kernel,
        out_shape=pltpu.HBM((steps, 512, width), jnp.bfloat16),
        in_specs=[pl.BlockSpec(memory_space=VMEM)],
        out_specs=pl.BlockSpec(memory_space=pltpu.HBM),
        scratch_shapes=[
            pltpu.VMEM((steps, 512, width), jnp.bfloat16),
            pltpu.SemaphoreType.DMA((steps,)),
        ],
        compiler_params=pltpu.CompilerParams(vmem_limit_bytes=10 << 20),
        cost_estimate=pl.CostEstimate(
            flops=2_000_000_000, bytes_accessed=6_400_000, transcendentals=0
        ),
        name="theory",
    )(flat)


def score_kernel(built, counts_ref, *refs):
    theories = refs[:built]
    flats = refs[built:4]
    own_ref, other_ref, out_ref = refs[4:7]
    scratch, (held, sems) = refs[7:-2], refs[-2:]
    copies = [
        pltpu.make_async_copy(theories[i].at[step], held.at[i, step], sems.at[i, step])
        for step in range(theories[0].shape[0])
        for i in range(built)
    ]
    for copy in copies:
        copy.start()
    y = lax.axis_index("spec") // 2
    core = lax.axis_index("spec") % 2
    mass = lax.axis_index("mass")
    steps = flats[0].shape[0]
    rows = own_ref.shape[0] * 2
    spectra = jnp.concatenate([own_ref[...], other_ref[...]], axis=0)
    slot = (iota((1, rows), 1) % SLOTS) // 2
    local = iota((512, 1), 0)

    def window(step, carry):
        best, total, square = carry
        live = counts_ref[mass * steps + step]
        for flat, place in zip(flats, scratch):
            theory_of(flat[step].astype(jnp.int32), place)
        for i in range(built):
            pltpu.make_async_copy(
                theories[i].at[step], held.at[i, step], sems.at[i, step]
            ).wait()
        now_best, now_total, now_square = [], [], []
        tables = [held.at[i, step] for i in range(built)] + list(scratch)
        for turn, theory in enumerate(tables):
            base = (((y + turn) % 4) * 2 + core) * 512
            scores = lax.dot_general(
                theory[...],
                spectra,
                (((1,), (1,)), ((), ())),
                preferred_element_type=jnp.float32,
            )
            valid = local < (live - base)
            now_best.append(jnp.max(jnp.where(valid, scores, -1e30), axis=0, keepdims=True))
            scores = jnp.where(valid, scores, 0.0)
            now_total.append(jnp.sum(scores, axis=0, keepdims=True))
            now_square.append(jnp.sum(scores * scores, axis=0, keepdims=True))
        here = slot == step
        best = jnp.where(here, functools.reduce(jnp.maximum, now_best), best)
        total = jnp.where(here, sum(now_total[1:], now_total[0]), total)
        square = jnp.where(here, sum(now_square[1:], now_square[0]), square)
        return best, total, square

    zeros = jnp.zeros((1, rows), jnp.float32)
    best, total, square = lax.fori_loop(0, steps, window, (zeros, zeros, zeros))
    stats = jnp.concatenate(
        [best / 32.0, total / 32.0, square / 1024.0, jnp.zeros((5, rows), jnp.float32)], axis=0
    )
    own, other = stats[:, : rows // 2], stats[:, rows // 2 :]
    first = jnp.where(core == 0, own, other)
    second = jnp.where(core == 0, other, own)
    peers = out_ref.shape[0] // 16
    for peer in range(peers):
        out_ref[peer * 8 : peer * 8 + 8, :] = first
        out_ref[(peers + peer) * 8 : (peers + peer) * 8 + 8, :] = second


def finish_kernel(counts_ref, routes_ref, stats_ref, best_ref, z_ref):
    rows = routes_ref.shape[1]
    mass = lax.axis_index("mass")
    windows = counts_ref.shape[1]
    picks = [routes_ref[0:1, :], routes_ref[1:2, :]]
    flat = jnp.concatenate(picks, axis=1)
    named_by = iota((windows, rows), 0)
    named = (picks[0] == named_by) | (picks[1] == named_by)
    before = jnp.where(iota((rows, rows), 0) < iota((rows, rows), 1), 1.0, 0.0)
    earlier = jnp.dot(
        jnp.where(named, 1.0, 0.0).astype(jnp.bfloat16),
        before.astype(jnp.bfloat16),
        preferred_element_type=jnp.float32,
    )
    slot = jnp.concatenate(
        [
            jnp.sum(jnp.where(pick == named_by, earlier, 0.0), axis=0, keepdims=True)
            for pick in picks
        ],
        axis=1,
    ).astype(jnp.int32)
    shard = flat // 3
    wanted = mass * SLOTS + (flat - shard * 3) * 2 + slot
    entries = 2 * rows
    lanes = stats_ref.shape[1]
    pick_lane = jnp.where(iota((lanes, entries), 0) == wanted, 1.0, 0.0)
    found = lax.dot_general(
        stats_ref[...],
        pick_lane,
        (((1,), (0,)), ((), ())),
        precision=lax.Precision.HIGHEST,
        preferred_element_type=jnp.float32,
    )
    peers = stats_ref.shape[0] // 16
    halves = []
    for half in range(2):
        chosen = jnp.zeros((8, entries), jnp.float32)
        for peer in range(peers):
            at = (half * peers + peer) * 8
            chosen = jnp.where(shard == peer, found[at : at + 8, :], chosen)
        halves.append(chosen)
    best = jnp.maximum(halves[0][0:1], halves[1][0:1])
    total = halves[0][1:2] + halves[1][1:2]
    square = halves[0][2:3] + halves[1][2:3]
    column = counts_ref[...].astype(jnp.float32)
    live = lax.dot_general(
        column,
        jnp.where(iota((windows, entries), 0) == flat, 1.0, 0.0),
        (((1,), (0,)), ((), ())),
        precision=lax.Precision.HIGHEST,
        preferred_element_type=jnp.float32,
    )
    mean = total / live
    spread = square / live - mean * mean
    z = (best - mean) / jnp.sqrt(spread + EPS)
    best_ref[0:1, :] = best[:, :rows]
    best_ref[1:2, :] = best[:, rows:]
    z_ref[0:1, :] = z[:, :rows]
    z_ref[1:2, :] = z[:, rows:]


def per_device(spectra, routes, pep_bins, counts):
    rows, width = spectra.shape
    mass_count = lax.axis_size("mass")
    spec_count = lax.axis_size("spec")
    steps = pep_bins.shape[0]
    routes_t = routes.T
    vmem = pl.BlockSpec(memory_space=VMEM)
    smem = pl.BlockSpec(memory_space=SMEM)
    hbm = pl.BlockSpec(memory_space=pltpu.HBM)
    outgoing, flat = pl.pallas_call(
        prepare_kernel,
        out_shape=(
            jax.ShapeDtypeStruct((mass_count * SLOTS, width), jnp.bfloat16),
            jax.ShapeDtypeStruct((steps, 128, 128), jnp.int16),
        ),
        in_specs=[hbm] * 3,
        out_specs=(vmem, vmem),
        scratch_shapes=[
            pltpu.VMEM((rows, width), spectra.dtype),
            pltpu.VMEM(routes_t.shape, routes_t.dtype),
            pltpu.VMEM(pep_bins.shape, pep_bins.dtype),
            pltpu.VMEM((rows, width + 2 * PAD), jnp.bfloat16),
            pltpu.VMEM((512, 128), jnp.int32),
            pltpu.SemaphoreType.DMA((3,)),
        ],
        compiler_params=pltpu.CompilerParams(vmem_limit_bytes=8 << 20),
        name="prepare",
    )(
        *[
            pltpu.with_memory_space_constraint(item, pltpu.HBM)
            for item in (spectra, routes_t, pep_bins)
        ]
    )
    flats = [flat] + [
        lax.ppermute(
            flat, "spec", [((i + 2 * turn) % spec_count, i) for i in range(spec_count)]
        )
        for turn in range(1, 4)
    ]
    own = lax.all_to_all(outgoing, "mass", split_axis=0, concat_axis=0, tiled=True)
    first = build_theory(flats[0], width)
    own, first, flats = lax.optimization_barrier((own, first, flats))
    other = lax.ppermute(own, "spec", [(i, i ^ 1) for i in range(spec_count)])
    theories = [first] + [build_theory(item, width) for item in flats[1:BUILT]]
    stats = pl.pallas_call(
        functools.partial(score_kernel, BUILT),
        out_shape=jax.ShapeDtypeStruct((2 * mass_count * 8, 128), jnp.float32),
        in_specs=[smem] + [hbm] * BUILT + [vmem] * (6 - BUILT),
        out_specs=vmem,
        scratch_shapes=[pltpu.VMEM((512, width), jnp.bfloat16)] * (4 - BUILT)
        + [
            pltpu.VMEM((BUILT, steps, 512, width), jnp.bfloat16),
            pltpu.SemaphoreType.DMA((BUILT, steps)),
        ],
        compiler_params=pltpu.CompilerParams(vmem_limit_bytes=32 << 20),
        name="score",
    )(
        counts,
        *[pltpu.with_memory_space_constraint(item, pltpu.HBM) for item in theories],
        *flats[BUILT:],
        own,
        other,
    )
    groups = [
        [(y * 2 + core) * mass_count + m for core in range(2) for m in range(mass_count)]
        for y in range(spec_count // 2)
    ]
    back = lax.all_to_all(
        stats,
        ("spec", "mass"),
        split_axis=0,
        concat_axis=0,
        tiled=True,
        axis_index_groups=groups,
    )
    best, z = pl.pallas_call(
        finish_kernel,
        out_shape=(jax.ShapeDtypeStruct((2, rows), jnp.float32),) * 2,
        in_specs=[vmem] * 3,
        out_specs=(vmem, vmem),
        name="finish",
    )(counts.reshape(1, -1), routes_t, back)
    return best.T, z.T


def solution(mesh):
    return jax.shard_map(
        per_device,
        mesh=mesh,
        in_specs=(
            P(("spec", "mass"), None),
            P(("spec", "mass"), None),
            P("mass", None, "spec"),
            P(),
        ),
        out_specs=(P(("spec", "mass"), None), P(("spec", "mass"), None)),
        check_vma=False,
    )
```

```python
import functools

import jax
import jax.numpy as jnp
from jax import lax
from jax.experimental import pallas as pl
from jax.experimental.pallas import tpu as pltpu
from jax.sharding import PartitionSpec as P

LAG = 75
EPS = 1e-06
PAD = 128
SLOTS = 8
LOW = 128
HIGH = 16
F8 = jnp.float8_e4m3fn
VMEM = pltpu.VMEM
SMEM = pltpu.SMEM


def iota(shape, axis):
    return lax.broadcasted_iota(jnp.int32, shape, axis)


def prepare_kernel(
    spectra_hbm,
    routes_hbm,
    pep_hbm,
    counts_hbm,
    out_hbm,
    flat_ref,
    where_hbm,
    out_ref,
    where_ref,
    counts_ref,
    spectra_ref,
    routes_ref,
    pep_ref,
    padded,
    turned,
    sems,
):
    copies = [
        pltpu.make_async_copy(spectra_hbm, spectra_ref, sems.at[0]),
        pltpu.make_async_copy(routes_hbm, routes_ref, sems.at[1]),
        pltpu.make_async_copy(pep_hbm, pep_ref, sems.at[2]),
        pltpu.make_async_copy(counts_hbm, counts_ref, sems.at[3]),
    ]
    for copy in copies:
        copy.start()
    rows, width = spectra_ref.shape
    block = 256
    gap = jnp.abs(iota((block + 2 * PAD, block), 0) - PAD - iota((block + 2 * PAD, block), 1))
    band = jnp.where((gap > 0) & (gap <= LAG), 1.0, 0.0).astype(jnp.bfloat16)
    copies[0].wait()
    rooted = jnp.sqrt(spectra_ref[...].astype(jnp.float32)).astype(jnp.bfloat16)
    padded[:, :PAD] = jnp.zeros((rows, PAD), jnp.bfloat16)
    padded[:, PAD + width :] = jnp.zeros((rows, PAD), jnp.bfloat16)
    padded[:, PAD : PAD + width] = rooted
    copies[1].wait()
    place = iota((out_ref.shape[0], rows), 0)
    inner = place % SLOTS
    window = (place // SLOTS) * 3 + inner // 2
    named = (routes_ref[0:1, :] == window) | (routes_ref[1:2, :] == window)
    named = named & (inner < 6)
    before = jnp.where(iota((rows, rows), 0) < iota((rows, rows), 1), 1.0, 0.0)
    earlier = jnp.dot(
        jnp.where(named, 1.0, 0.0).astype(jnp.bfloat16),
        before.astype(jnp.bfloat16),
        preferred_element_type=jnp.float32,
    )
    taken = named & (earlier == (inner % 2).astype(jnp.float32))
    routing = jnp.where(taken, 1.0, 0.0).astype(jnp.bfloat16)
    leaving = []
    for start in range(0, width, block):
        background = jnp.dot(
            padded[:, start : start + block + 2 * PAD], band, preferred_element_type=jnp.float32
        )
        values = rooted[:, start : start + block].astype(jnp.float32)
        prepared = (values - background / (2.0 * LAG)).astype(jnp.bfloat16)
        out_ref[:, start : start + block] = jnp.dot(
            routing, prepared, preferred_element_type=jnp.float32
        ).astype(jnp.bfloat16)
        columns = pl.ds(start, block)
        leaving.append(
            pltpu.make_async_copy(
                out_ref.at[:, columns], out_hbm.at[:, columns], sems.at[5 + start // block]
            )
        )
        leaving[-1].start()
    copies[3].wait()
    mass = lax.axis_index("mass")
    windows = counts_ref.shape[0]
    counted = jnp.zeros((windows, rows), jnp.int32)
    at_window = iota((windows, rows), 0)
    for index in range(windows):
        counted = jnp.where(at_window == index, counts_ref[index], counted)
    where_ref[...] = jnp.zeros_like(where_ref)
    for pick in range(2):
        here = routes_ref[pick : pick + 1, :]
        mine = taken & (window == here)
        found = jnp.sum(jnp.where(mine, place, 0), axis=0, keepdims=True)
        lanes = slice(pick * rows, (pick + 1) * rows)
        where_ref[0:1, lanes] = mass * SLOTS + found % SLOTS
        where_ref[1:2, lanes] = found // SLOTS
        where_ref[2:3, lanes] = jnp.sum(
            jnp.where(at_window == here, counted, 0), axis=0, keepdims=True
        )
    leaving.append(pltpu.make_async_copy(where_ref, where_hbm, sems.at[4]))
    leaving[-1].start()
    copies[2].wait()
    lane = iota((128, 128), 1) // 32
    for step in range(pep_ref.shape[0]):
        table = pep_ref[step]
        turned[...] = jnp.concatenate([table] * 4, axis=0).T
        flat = jnp.zeros((128, 128), jnp.int32)
        for part in range(4):
            flat = jnp.where(lane == part, turned[pl.ds(part, 128, stride=4), :], flat)
        flat_ref[step] = flat.astype(jnp.int16)
    for copy in leaving:
        copy.wait()


def theory_of(bins, theory_ref, finished=None):
    width = bins.shape[1]
    high_place = iota((HIGH * 8, 2 * width), 0).astype(jnp.float32).astype(jnp.bfloat16)
    low_place = iota((LOW, 2 * width), 0).astype(jnp.float32).astype(jnp.bfloat16)
    one = jnp.ones((), F8)
    zero = jnp.zeros((), F8)
    member = iota((128, 128), 1) // 32 + 4 * (iota((128, 128), 0) % 2)
    low = (bins & (LOW - 1)).astype(jnp.float32).astype(jnp.bfloat16)
    high = ((bins >> 7) * 8 + member).astype(jnp.float32).astype(jnp.bfloat16)
    for pair in range(32):
        parts = []
        for half in range(2):
            row = 4 * pair + 2 * half
            high_row = jnp.concatenate([high[row : row + 1], high[row + 1 : row + 2]], axis=1)
            low_row = jnp.concatenate([low[row : row + 1], low[row + 1 : row + 2]], axis=1)
            parts.append(
                lax.dot_general(
                    jnp.where(high_place == high_row, one, zero),
                    jnp.where(low_place == low_row, one, zero),
                    (((1,), (1,)), ((), ())),
                    preferred_element_type=jnp.float32,
                )
            )
        for part in range(HIGH):
            tile = jnp.concatenate([item[part * 8 : part * 8 + 8] for item in parts], axis=0)
            theory_ref[pair * 16 : pair * 16 + 16, part * LOW : (part + 1) * LOW] = tile.astype(
                jnp.bfloat16
            )
        if finished is not None and pair % 8 == 7:
            finished(pair // 8)


def theory_kernel(flat_ref, theory_ref):
    def window(step, carry):
        theory_of(flat_ref[step].astype(jnp.int32), theory_ref.at[step])
        return carry

    lax.fori_loop(0, flat_ref.shape[0], window, 0)


def stored_theory_kernel(flat_ref, theory_ref, held, sems):
    steps = flat_ref.shape[0]

    def copy_of(step, quarter):
        rows = pl.ds(quarter * 128, 128)
        return pltpu.make_async_copy(
            held.at[step, rows], theory_ref.at[step, rows], sems.at[step, quarter]
        )

    def window(step, carry):
        theory_of(
            flat_ref[step].astype(jnp.int32),
            held.at[step],
            lambda quarter: copy_of(step, quarter).start(),
        )
        return carry

    lax.fori_loop(0, steps, window, 0)
    for step in range(steps):
        for quarter in range(4):
            copy_of(step, quarter).wait()


def build_theory(flat, width, stored):
    steps = flat.shape[0]
    shape = (steps, 512, width)
    space = pltpu.HBM if stored else VMEM
    scratch = [pltpu.VMEM(shape, jnp.bfloat16), pltpu.SemaphoreType.DMA((steps, 4))]
    return pl.pallas_call(
        stored_theory_kernel if stored else theory_kernel,
        out_shape=space(shape, jnp.bfloat16),
        in_specs=[pl.BlockSpec(memory_space=VMEM)],
        out_specs=pl.BlockSpec(memory_space=space),
        scratch_shapes=scratch if stored else [],
        compiler_params=pltpu.CompilerParams(vmem_limit_bytes=(10 if stored else 4) << 20),
        cost_estimate=pl.CostEstimate(
            flops=2_000_000_000, bytes_accessed=6_400_000, transcendentals=0
        ),
        name="theory",
    )(flat)


def score_kernel(
    counts_ref,
    stored_ref,
    theory_ref,
    flat2_ref,
    flat3_ref,
    own_ref,
    other_ref,
    out_ref,
    held,
    built2,
    built3,
    sems,
):
    steps = theory_ref.shape[0]

    def copy_of(step):
        return pltpu.make_async_copy(stored_ref.at[step], held.at[step], sems.at[step])

    for step in range(steps):
        copy_of(step).start()
    y = lax.axis_index("spec") // 2
    core = lax.axis_index("spec") % 2
    mass = lax.axis_index("mass")
    rows = own_ref.shape[0] * 2
    spectra = jnp.concatenate([own_ref[...], other_ref[...]], axis=0)
    slot = (iota((1, rows), 1) % SLOTS) // 2
    local = iota((512, 1), 0)

    def window(step, carry):
        best, total, square = carry
        live = counts_ref[mass * steps + step]
        theory_of(flat2_ref[step].astype(jnp.int32), built2)
        theory_of(flat3_ref[step].astype(jnp.int32), built3)
        copy_of(step).wait()
        now_best, now_total, now_square = [], [], []
        tables = [held.at[step], theory_ref.at[step], built2, built3]
        for turn, theory in enumerate(tables):
            base = (((y + turn) % 4) * 2 + core) * 512
            scores = lax.dot_general(
                theory[...],
                spectra,
                (((1,), (1,)), ((), ())),
                preferred_element_type=jnp.float32,
            )
            valid = local < (live - base)
            now_best.append(jnp.max(jnp.where(valid, scores, -1e30), axis=0, keepdims=True))
            scores = jnp.where(valid, scores, 0.0)
            now_total.append(jnp.sum(scores, axis=0, keepdims=True))
            now_square.append(jnp.sum(scores * scores, axis=0, keepdims=True))
        here = slot == step
        best = jnp.where(here, functools.reduce(jnp.maximum, now_best), best)
        total = jnp.where(here, sum(now_total[1:], now_total[0]), total)
        square = jnp.where(here, sum(now_square[1:], now_square[0]), square)
        return best, total, square

    zeros = jnp.zeros((1, rows), jnp.float32)
    best, total, square = lax.fori_loop(0, steps, window, (zeros, zeros, zeros))
    stats = jnp.concatenate(
        [best / 32.0, total / 32.0, square / 1024.0, jnp.zeros((5, rows), jnp.float32)], axis=0
    )
    own, other = stats[:, : rows // 2], stats[:, rows // 2 :]
    first = jnp.where(core == 0, own, other)
    second = jnp.where(core == 0, other, own)
    peers = out_ref.shape[0] // 16
    for peer in range(peers):
        out_ref[peer * 8 : peer * 8 + 8, :] = first
        out_ref[(peers + peer) * 8 : (peers + peer) * 8 + 8, :] = second


def finish_kernel(where_hbm, stats_hbm, best_ref, z_ref, where_ref, stats_ref, sems):
    copies = [
        pltpu.make_async_copy(stats_hbm, stats_ref, sems.at[0]),
        pltpu.make_async_copy(where_hbm, where_ref, sems.at[1]),
    ]
    for copy in copies:
        copy.start()
    for copy in copies:
        copy.wait()
    rows = best_ref.shape[1]
    peers = stats_ref.shape[0] // 16
    lane = jnp.broadcast_to(where_ref[0:1, :], (8, 128))
    shard = where_ref[1:2, :]
    live = where_ref[2:3, :].astype(jnp.float32)
    halves = []
    for half in range(2):
        chosen = jnp.zeros((8, 128), jnp.float32)
        for peer in range(peers):
            at = (half * peers + peer) * 8
            found = jnp.take_along_axis(stats_ref[at : at + 8, :], lane, axis=1)
            chosen = jnp.where(shard == peer, found, chosen)
        halves.append(chosen)
    best = jnp.maximum(halves[0][0:1], halves[1][0:1])
    total = halves[0][1:2] + halves[1][1:2]
    square = halves[0][2:3] + halves[1][2:3]
    mean = total / live
    spread = square / live - mean * mean
    z = (best - mean) / jnp.sqrt(spread + EPS)
    best_ref[0:1, :] = best[:, :rows]
    best_ref[1:2, :] = best[:, rows : 2 * rows]
    z_ref[0:1, :] = z[:, :rows]
    z_ref[1:2, :] = z[:, rows : 2 * rows]


def per_device(spectra, routes, pep_bins, counts):
    rows, width = spectra.shape
    mass_count = lax.axis_size("mass")
    spec_count = lax.axis_size("spec")
    steps = pep_bins.shape[0]
    routes_t = routes.T
    vmem = pl.BlockSpec(memory_space=VMEM)
    smem = pl.BlockSpec(memory_space=SMEM)
    hbm = pl.BlockSpec(memory_space=pltpu.HBM)
    outgoing, flat, where = pl.pallas_call(
        prepare_kernel,
        out_shape=(
            pltpu.HBM((mass_count * SLOTS, width), jnp.bfloat16),
            jax.ShapeDtypeStruct((steps, 128, 128), jnp.int16),
            pltpu.HBM((8, 128), jnp.int32),
        ),
        in_specs=[hbm] * 4,
        out_specs=(hbm, vmem, hbm),
        scratch_shapes=[
            pltpu.VMEM((mass_count * SLOTS, width), jnp.bfloat16),
            pltpu.VMEM((8, 128), jnp.int32),
            pltpu.SMEM(counts.shape, counts.dtype),
            pltpu.VMEM((rows, width), spectra.dtype),
            pltpu.VMEM(routes_t.shape, routes_t.dtype),
            pltpu.VMEM(pep_bins.shape, pep_bins.dtype),
            pltpu.VMEM((rows, width + 2 * PAD), jnp.bfloat16),
            pltpu.VMEM((512, 128), jnp.int32),
            pltpu.SemaphoreType.DMA((5 + width // 256,)),
        ],
        compiler_params=pltpu.CompilerParams(vmem_limit_bytes=8 << 20),
        name="prepare",
    )(
        *[
            pltpu.with_memory_space_constraint(item, pltpu.HBM)
            for item in (spectra, routes_t, pep_bins, counts)
        ]
    )
    flats = [flat] + [
        lax.ppermute(
            flat, "spec", [((i + 2 * turn) % spec_count, i) for i in range(spec_count)]
        )
        for turn in range(1, 4)
    ]
    own = lax.all_to_all(outgoing, "mass", split_axis=0, concat_axis=0, tiled=True)
    first = build_theory(flats[0], width, True)
    own, first, flats = lax.optimization_barrier((own, first, flats))
    other = lax.ppermute(own, "spec", [(i, i ^ 1) for i in range(spec_count)])
    second = build_theory(flats[1], width, False)
    stats = pl.pallas_call(
        score_kernel,
        out_shape=jax.ShapeDtypeStruct((2 * mass_count * 8, 128), jnp.float32),
        in_specs=[smem, hbm] + [vmem] * 5,
        out_specs=vmem,
        scratch_shapes=[
            pltpu.VMEM((steps, 512, width), jnp.bfloat16),
            pltpu.VMEM((512, width), jnp.bfloat16),
            pltpu.VMEM((512, width), jnp.bfloat16),
            pltpu.SemaphoreType.DMA((steps,)),
        ],
        compiler_params=pltpu.CompilerParams(vmem_limit_bytes=24 << 20),
        name="score",
    )(
        counts,
        pltpu.with_memory_space_constraint(first, pltpu.HBM),
        second,
        flats[2],
        flats[3],
        own,
        other,
    )
    groups = [
        [(y * 2 + core) * mass_count + m for core in range(2) for m in range(mass_count)]
        for y in range(spec_count // 2)
    ]
    back = lax.all_to_all(
        stats,
        ("spec", "mass"),
        split_axis=0,
        concat_axis=0,
        tiled=True,
        axis_index_groups=groups,
    )
    best, z = pl.pallas_call(
        finish_kernel,
        out_shape=(jax.ShapeDtypeStruct((2, rows), jnp.float32),) * 2,
        in_specs=[hbm] * 2,
        out_specs=(vmem, vmem),
        scratch_shapes=[
            pltpu.VMEM((8, 128), jnp.int32),
            pltpu.VMEM(back.shape, jnp.float32),
            pltpu.SemaphoreType.DMA((2,)),
        ],
        name="finish",
    )(*[pltpu.with_memory_space_constraint(item, pltpu.HBM) for item in (where, back)])
    return best.T, z.T


def solution(mesh):
    return jax.shard_map(
        per_device,
        mesh=mesh,
        in_specs=(
            P(("spec", "mass"), None),
            P(("spec", "mass"), None),
            P("mass", None, "spec"),
            P(),
        ),
        out_specs=(P(("spec", "mass"), None), P(("spec", "mass"), None)),
        check_vma=False,
    )
```

```python
import functools

import jax
import jax.numpy as jnp
from jax import lax
from jax.experimental import pallas as pl
from jax.experimental.pallas import tpu as pltpu
from jax.sharding import PartitionSpec as P

LAG = 75
EPS = 1e-06
PAD = 128
SLOTS = 8
LOW = 128
HIGH = 16
F8 = jnp.float8_e4m3fn
VMEM = pltpu.VMEM
SMEM = pltpu.SMEM


def iota(shape, axis):
    return lax.broadcasted_iota(jnp.int32, shape, axis)


def prepare_kernel(
    spectra_hbm,
    routes_hbm,
    pep_hbm,
    counts_hbm,
    out_hbm,
    flat_ref,
    where_hbm,
    out_ref,
    where_ref,
    counts_ref,
    spectra_ref,
    routes_ref,
    pep_ref,
    padded,
    turned,
    sems,
):
    copies = [
        pltpu.make_async_copy(spectra_hbm, spectra_ref, sems.at[0]),
        pltpu.make_async_copy(routes_hbm, routes_ref, sems.at[1]),
        pltpu.make_async_copy(pep_hbm, pep_ref, sems.at[2]),
        pltpu.make_async_copy(counts_hbm, counts_ref, sems.at[3]),
    ]
    for copy in copies:
        copy.start()
    rows, width = spectra_ref.shape
    block = 256
    gap = jnp.abs(iota((block + 2 * PAD, block), 0) - PAD - iota((block + 2 * PAD, block), 1))
    band = jnp.where((gap > 0) & (gap <= LAG), 1.0, 0.0).astype(jnp.bfloat16)
    copies[0].wait()
    rooted = jnp.sqrt(spectra_ref[...].astype(jnp.float32)).astype(jnp.bfloat16)
    padded[:, :PAD] = jnp.zeros((rows, PAD), jnp.bfloat16)
    padded[:, PAD + width :] = jnp.zeros((rows, PAD), jnp.bfloat16)
    padded[:, PAD : PAD + width] = rooted
    peak = jnp.max(rooted.astype(jnp.float32), axis=1, keepdims=True)
    scale = jnp.ones((rows, 1), jnp.float32)
    for power in (16, 8, 4, 2, 1):
        larger = scale * 2.0**power
        scale = jnp.where(peak * larger <= 256.0, larger, scale)
    copies[1].wait()
    place = iota((out_ref.shape[0], rows), 0)
    inner = place % SLOTS
    window = (place // SLOTS) * 3 + inner // 2
    named = (routes_ref[0:1, :] == window) | (routes_ref[1:2, :] == window)
    named = named & (inner < 6)
    before = jnp.where(iota((rows, rows), 0) < iota((rows, rows), 1), 1.0, 0.0)
    earlier = jnp.dot(
        jnp.where(named, 1.0, 0.0).astype(jnp.bfloat16),
        before.astype(jnp.bfloat16),
        preferred_element_type=jnp.float32,
    )
    taken = named & (earlier == (inner % 2).astype(jnp.float32))
    routing = jnp.where(taken, 1.0, 0.0).astype(jnp.bfloat16)
    leaving = []
    for start in range(0, width, block):
        background = jnp.dot(
            padded[:, start : start + block + 2 * PAD], band, preferred_element_type=jnp.float32
        )
        values = rooted[:, start : start + block].astype(jnp.float32)
        prepared = (values - background / (2.0 * LAG)).astype(jnp.bfloat16)
        prepared = (prepared.astype(jnp.float32) * scale).astype(jnp.bfloat16)
        out_ref[:, start : start + block] = jnp.dot(
            routing, prepared, preferred_element_type=jnp.float32
        ).astype(jnp.bfloat16)
        columns = pl.ds(start, block)
        leaving.append(
            pltpu.make_async_copy(
                out_ref.at[:, columns], out_hbm.at[:, columns], sems.at[5 + start // block]
            )
        )
        leaving[-1].start()
    copies[3].wait()
    mass = lax.axis_index("mass")
    windows = counts_ref.shape[0]
    counted = jnp.zeros((windows, rows), jnp.float32)
    at_window = iota((windows, rows), 0)
    for index in range(windows):
        counted = jnp.where(at_window == index, counts_ref[index].astype(jnp.float32), counted)
    where_ref[...] = jnp.zeros_like(where_ref)
    diagonal = iota((rows, rows), 0) == iota((rows, rows), 1)
    turned_scale = jnp.sum(jnp.where(diagonal, scale, 0.0), axis=0, keepdims=True)
    for pick in range(2):
        here = routes_ref[pick : pick + 1, :]
        mine = taken & (window == here)
        found = jnp.sum(jnp.where(mine, place, 0), axis=0, keepdims=True)
        lanes = slice(pick * rows, (pick + 1) * rows)
        inside = found % SLOTS
        where_ref[0:1, lanes] = ((inside // 2) * 32 + mass * 2 + inside % 2).astype(jnp.float32)
        where_ref[1:2, lanes] = (found // SLOTS).astype(jnp.float32)
        where_ref[2:3, lanes] = jnp.sum(
            jnp.where(at_window == here, counted, 0.0), axis=0, keepdims=True
        )
        where_ref[3:4, lanes] = turned_scale
    leaving.append(pltpu.make_async_copy(where_ref, where_hbm, sems.at[4]))
    leaving[-1].start()
    copies[2].wait()
    lane = iota((128, 128), 1) // 32
    for step in range(pep_ref.shape[0]):
        table = pep_ref[step]
        turned[...] = jnp.concatenate([table] * 4, axis=0).T
        flat = jnp.zeros((128, 128), jnp.int32)
        for part in range(4):
            flat = jnp.where(lane == part, turned[pl.ds(part, 128, stride=4), :], flat)
        flat_ref[step] = flat.astype(jnp.int16)
    for copy in leaving:
        copy.wait()


def theory_of(bins, theory_ref, finished=None):
    width = bins.shape[1]
    high_place = iota((HIGH * 8, 2 * width), 0).astype(jnp.float32).astype(jnp.bfloat16)
    low_place = iota((LOW, 2 * width), 0).astype(jnp.float32).astype(jnp.bfloat16)
    one = jnp.ones((), F8)
    zero = jnp.zeros((), F8)
    member = iota((128, 128), 1) // 32 + 4 * (iota((128, 128), 0) % 2)
    low = (bins & (LOW - 1)).astype(jnp.float32).astype(jnp.bfloat16)
    high = ((bins >> 7) * 8 + member).astype(jnp.float32).astype(jnp.bfloat16)
    largest = jnp.zeros((8, 128), jnp.float32)
    for quad in range(16):
        parts = []
        for item in range(4):
            row = 8 * quad + 2 * item
            high_row = jnp.concatenate([high[row : row + 1], high[row + 1 : row + 2]], axis=1)
            low_row = jnp.concatenate([low[row : row + 1], low[row + 1 : row + 2]], axis=1)
            parts.append(
                lax.dot_general(
                    jnp.where(high_place == high_row, one, zero),
                    jnp.where(low_place == low_row, one, zero),
                    (((1,), (1,)), ((), ())),
                    preferred_element_type=jnp.float32,
                )
            )
        for part in range(HIGH):
            pieces = [item[part * 8 : part * 8 + 8] for item in parts]
            theory_ref[quad * 32 : quad * 32 + 32, part * LOW : (part + 1) * LOW] = (
                jnp.concatenate(pieces, axis=0).astype(theory_ref.dtype)
            )
            more = jnp.maximum(
                jnp.maximum(pieces[0], pieces[1]), jnp.maximum(pieces[2], pieces[3])
            )
            largest = jnp.maximum(largest, more)
        if finished is not None and quad % 4 == 3:
            finished(quad // 4)
    return largest


def theory_kernel(flat_ref, theory_ref, largest_ref):
    def window(step, carry):
        largest_ref[step] = theory_of(flat_ref[step].astype(jnp.int32), theory_ref.at[step])
        return carry

    lax.fori_loop(0, flat_ref.shape[0], window, 0)


def stored_theory_kernel(flat_ref, theory_hbm, largest_hbm, held, largest, sems):
    steps = flat_ref.shape[0]

    def copy_of(step, quarter):
        rows = pl.ds(quarter * 128, 128)
        return pltpu.make_async_copy(
            held.at[step, rows], theory_hbm.at[step, rows], sems.at[step, quarter]
        )

    def window(step, carry):
        largest[step] = theory_of(
            flat_ref[step].astype(jnp.int32),
            held.at[step],
            lambda quarter: copy_of(step, quarter).start(),
        )
        return carry

    lax.fori_loop(0, steps, window, 0)
    last = pltpu.make_async_copy(largest, largest_hbm, sems.at[steps, 0])
    last.start()
    for step in range(steps):
        for quarter in range(4):
            copy_of(step, quarter).wait()
    last.wait()


def build_theory(flat, width, stored):
    steps = flat.shape[0]
    shape, small = (steps, 512, width), (steps, 8, 128)
    space = pltpu.HBM if stored else VMEM
    scratch = [
        pltpu.VMEM(shape, F8),
        pltpu.VMEM(small, jnp.float32),
        pltpu.SemaphoreType.DMA((steps + 1, 4)),
    ]
    return pl.pallas_call(
        stored_theory_kernel if stored else theory_kernel,
        out_shape=(space(shape, F8), space(small, jnp.float32)),
        in_specs=[pl.BlockSpec(memory_space=VMEM)],
        out_specs=(pl.BlockSpec(memory_space=space),) * 2,
        scratch_shapes=scratch if stored else [],
        compiler_params=pltpu.CompilerParams(vmem_limit_bytes=(8 if stored else 4) << 20),
        cost_estimate=pl.CostEstimate(
            flops=2_000_000_000, bytes_accessed=6_400_000, transcendentals=0
        ),
        name="theory",
    )(flat)


def score_kernel(
    counts_ref,
    stored_hbm,
    stored_largest_hbm,
    theory_ref,
    largest_ref,
    flat0_ref,
    flat1_ref,
    flat2_ref,
    flat3_ref,
    own_ref,
    other_ref,
    out_ref,
    held,
    held_largest,
    built2,
    built3,
    halves,
    stats_ref,
    exact,
    tables_ref,
    sems,
):
    steps, width = theory_ref.shape[0], theory_ref.shape[2]
    flats = (flat0_ref, flat1_ref, flat2_ref, flat3_ref)

    def copy_of(step):
        return pltpu.make_async_copy(stored_hbm.at[step], held.at[step], sems.at[step])

    small = pltpu.make_async_copy(stored_largest_hbm, held_largest, sems.at[steps])
    small.start()
    for step in range(steps):
        copy_of(step).start()
    y = lax.axis_index("spec") // 2
    core = lax.axis_index("spec") % 2
    mass = lax.axis_index("mass")
    rows = own_ref.shape[0]
    local = iota((512, 1), 0)
    entry = iota((64, rows), 0) % 32
    source = (entry // 2) * SLOTS + entry % 2
    first_half = iota((64, rows), 0) < 32

    def chosen(step):
        mine = iota((64, rows), 1) == source + 2 * step
        return sum(
            jnp.dot(
                jnp.where(mine & (first_half == first), 1.0, 0.0).astype(jnp.bfloat16),
                ref[...],
                preferred_element_type=jnp.float32,
            )
            for first, ref in ((True, own_ref), (False, other_ref))
        )

    for step in range(steps):
        values = chosen(step)
        upper = values.astype(F8)
        halves[step, :64, :] = upper
        halves[step, 64:, :] = (values - upper.astype(jnp.float32)).astype(F8)
    small.wait()

    def reduced(scores, limit):
        valid = local < limit
        best = jnp.max(jnp.where(valid, scores, -1e30), axis=0, keepdims=True)
        scores = jnp.where(valid, scores, 0.0)
        return (
            best,
            jnp.sum(scores, axis=0, keepdims=True),
            jnp.sum(scores * scores, axis=0, keepdims=True),
        )

    def base_of(turn):
        return (lax.rem(y + turn, 4) * 2 + core) * 512

    def keep(step, found):
        stats_ref[step, 0:1, :] = functools.reduce(jnp.maximum, [item[0] for item in found])
        for row in (1, 2):
            stats_ref[step, row : row + 1, :] = functools.reduce(
                jnp.add, [item[row] for item in found]
            )

    def window(step, carry):
        live = counts_ref[mass * steps + step]
        largest = jnp.maximum(
            theory_of(flat2_ref[step].astype(jnp.int32), built2),
            theory_of(flat3_ref[step].astype(jnp.int32), built3),
        )
        largest = jnp.maximum(largest, jnp.maximum(held_largest[step], largest_ref[step]))
        beyond = jnp.max(largest) > 16.0
        copy_of(step).wait()
        found = []
        for turn, theory in enumerate((held.at[step], theory_ref.at[step], built2, built3)):
            scores = lax.dot_general(
                theory[...],
                halves[step],
                (((1,), (1,)), ((), ())),
                preferred_element_type=jnp.float32,
            )
            scores = scores + pltpu.roll(scores, 64, 1)
            found.append(reduced(scores, live - base_of(turn)))
        keep(step, found)

        @pl.when(beyond)
        def _():
            for turn in range(4):
                tables_ref[turn] = flats[turn][step].astype(jnp.int32)
            values = chosen(step).astype(jnp.bfloat16)
            values = jnp.concatenate([values, jnp.zeros_like(values)], axis=0)

            def piece(turn, found):
                theory_of(tables_ref[turn], exact)
                scores = lax.dot_general(
                    exact[...],
                    values,
                    (((1,), (1,)), ((), ())),
                    preferred_element_type=jnp.float32,
                )
                more = reduced(scores, live - base_of(turn))
                return (
                    jnp.maximum(found[0], more[0]),
                    found[1] + more[1],
                    found[2] + more[2],
                )

            zeros = jnp.zeros((1, 128), jnp.float32)
            keep(step, [lax.fori_loop(0, 4, piece, (zeros - 1e30, zeros, zeros))])

        return carry

    stats_ref[...] = jnp.zeros_like(stats_ref)
    lax.fori_loop(0, steps, window, 0)
    part = iota((8, 128), 1) // 32
    tiles = []
    for half in range(2):
        tile = jnp.zeros((8, 128), jnp.float32)
        for step in range(steps):
            moved = pltpu.roll(stats_ref[step], (step * 32 - half * 32) % 128, 1)
            tile = jnp.where(part == step, moved, tile)
        tiles.append(tile)
    first = jnp.where(core == 0, tiles[0], tiles[1])
    second = jnp.where(core == 0, tiles[1], tiles[0])
    peers = out_ref.shape[0] // 16
    for peer in range(peers):
        out_ref[peer * 8 : peer * 8 + 8, :] = first
        out_ref[(peers + peer) * 8 : (peers + peer) * 8 + 8, :] = second


def finish_kernel(where_hbm, stats_hbm, best_ref, z_ref, where_ref, stats_ref, sems):
    copies = [
        pltpu.make_async_copy(stats_hbm, stats_ref, sems.at[0]),
        pltpu.make_async_copy(where_hbm, where_ref, sems.at[1]),
    ]
    for copy in copies:
        copy.start()
    for copy in copies:
        copy.wait()
    rows = best_ref.shape[1]
    peers = stats_ref.shape[0] // 16
    lane = jnp.broadcast_to(where_ref[0:1, :].astype(jnp.int32), (8, 128))
    shard = where_ref[1:2, :].astype(jnp.int32)
    live = where_ref[2:3, :]
    unscale = 1.0 / (where_ref[3:4, :] * 32.0)
    halves = []
    for half in range(2):
        chosen = jnp.zeros((8, 128), jnp.float32)
        for peer in range(peers):
            at = (half * peers + peer) * 8
            found = jnp.take_along_axis(stats_ref[at : at + 8, :], lane, axis=1)
            chosen = jnp.where(shard == peer, found, chosen)
        halves.append(chosen)
    best = jnp.maximum(halves[0][0:1], halves[1][0:1]) * unscale
    total = (halves[0][1:2] + halves[1][1:2]) * unscale
    square = (halves[0][2:3] + halves[1][2:3]) * unscale * unscale
    mean = total / live
    spread = square / live - mean * mean
    z = (best - mean) / jnp.sqrt(spread + EPS)
    best_ref[0:1, :] = best[:, :rows]
    best_ref[1:2, :] = best[:, rows : 2 * rows]
    z_ref[0:1, :] = z[:, :rows]
    z_ref[1:2, :] = z[:, rows : 2 * rows]


def per_device(spectra, routes, pep_bins, counts):
    rows, width = spectra.shape
    mass_count = lax.axis_size("mass")
    spec_count = lax.axis_size("spec")
    steps = pep_bins.shape[0]
    routes_t = routes.T
    vmem = pl.BlockSpec(memory_space=VMEM)
    smem = pl.BlockSpec(memory_space=SMEM)
    hbm = pl.BlockSpec(memory_space=pltpu.HBM)
    outgoing, flat, where = pl.pallas_call(
        prepare_kernel,
        out_shape=(
            pltpu.HBM((mass_count * SLOTS, width), jnp.bfloat16),
            jax.ShapeDtypeStruct((steps, 128, 128), jnp.int16),
            pltpu.HBM((8, 128), jnp.float32),
        ),
        in_specs=[hbm] * 4,
        out_specs=(hbm, vmem, hbm),
        scratch_shapes=[
            pltpu.VMEM((mass_count * SLOTS, width), jnp.bfloat16),
            pltpu.VMEM((8, 128), jnp.float32),
            pltpu.SMEM(counts.shape, counts.dtype),
            pltpu.VMEM((rows, width), spectra.dtype),
            pltpu.VMEM(routes_t.shape, routes_t.dtype),
            pltpu.VMEM(pep_bins.shape, pep_bins.dtype),
            pltpu.VMEM((rows, width + 2 * PAD), jnp.bfloat16),
            pltpu.VMEM((512, 128), jnp.int32),
            pltpu.SemaphoreType.DMA((5 + width // 256,)),
        ],
        compiler_params=pltpu.CompilerParams(vmem_limit_bytes=8 << 20),
        name="prepare",
    )(
        *[
            pltpu.with_memory_space_constraint(item, pltpu.HBM)
            for item in (spectra, routes_t, pep_bins, counts)
        ]
    )
    flats = [flat] + [
        lax.ppermute(
            flat, "spec", [((i + 2 * turn) % spec_count, i) for i in range(spec_count)]
        )
        for turn in range(1, 4)
    ]
    own = lax.all_to_all(outgoing, "mass", split_axis=0, concat_axis=0, tiled=True)
    first, first_largest = build_theory(flats[0], width, True)
    own, first, flats = lax.optimization_barrier((own, first, flats))
    other = lax.ppermute(own, "spec", [(i, i ^ 1) for i in range(spec_count)])
    second, second_largest = build_theory(flats[1], width, False)
    stats = pl.pallas_call(
        score_kernel,
        out_shape=jax.ShapeDtypeStruct((2 * mass_count * 8, 128), jnp.float32),
        in_specs=[smem, hbm, hbm] + [vmem] * 8,
        out_specs=vmem,
        scratch_shapes=[
            pltpu.VMEM((steps, 512, width), F8),
            pltpu.VMEM((steps, 8, 128), jnp.float32),
            pltpu.VMEM((512, width), F8),
            pltpu.VMEM((512, width), F8),
            pltpu.VMEM((steps, 128, width), F8),
            pltpu.VMEM((steps, 8, 128), jnp.float32),
            pltpu.VMEM((512, width), jnp.bfloat16),
            pltpu.VMEM((4, 128, 128), jnp.int32),
            pltpu.SemaphoreType.DMA((steps + 1,)),
        ],
        compiler_params=pltpu.CompilerParams(vmem_limit_bytes=24 << 20),
        name="score",
    )(
        counts,
        pltpu.with_memory_space_constraint(first, pltpu.HBM),
        pltpu.with_memory_space_constraint(first_largest, pltpu.HBM),
        second,
        second_largest,
        *flats,
        own,
        other,
    )
    groups = [
        [(y * 2 + core) * mass_count + m for core in range(2) for m in range(mass_count)]
        for y in range(spec_count // 2)
    ]
    back = lax.all_to_all(
        stats,
        ("spec", "mass"),
        split_axis=0,
        concat_axis=0,
        tiled=True,
        axis_index_groups=groups,
    )
    best, z = pl.pallas_call(
        finish_kernel,
        out_shape=(jax.ShapeDtypeStruct((2, rows), jnp.float32),) * 2,
        in_specs=[hbm] * 2,
        out_specs=(vmem, vmem),
        scratch_shapes=[
            pltpu.VMEM((8, 128), jnp.float32),
            pltpu.VMEM(back.shape, jnp.float32),
            pltpu.SemaphoreType.DMA((2,)),
        ],
        name="finish",
    )(*[pltpu.with_memory_space_constraint(item, pltpu.HBM) for item in (where, back)])
    return best.T, z.T


def solution(mesh):
    return jax.shard_map(
        per_device,
        mesh=mesh,
        in_specs=(
            P(("spec", "mass"), None),
            P(("spec", "mass"), None),
            P("mass", None, "spec"),
            P(),
        ),
        out_specs=(P(("spec", "mass"), None), P(("spec", "mass"), None)),
        check_vma=False,
    )
```

```python
import functools

import jax
import jax.numpy as jnp
from jax import lax
from jax.experimental import pallas as pl
from jax.experimental.pallas import tpu as pltpu
from jax.sharding import PartitionSpec as P

LAG = 75
EPS = 1e-06
PAD = 128
SLOTS = 8
LOW = 128
HIGH = 16
F8 = jnp.float8_e4m3fn
VMEM = pltpu.VMEM
SMEM = pltpu.SMEM


def iota(shape, axis):
    return lax.broadcasted_iota(jnp.int32, shape, axis)


def prepare_kernel(
    spectra_hbm,
    routes_hbm,
    pep_hbm,
    counts_hbm,
    out_hbm,
    flat_ref,
    where_hbm,
    out_ref,
    where_ref,
    counts_ref,
    spectra_ref,
    routes_ref,
    pep_ref,
    padded,
    sems,
):
    copies = [
        pltpu.make_async_copy(spectra_hbm, spectra_ref, sems.at[0]),
        pltpu.make_async_copy(routes_hbm, routes_ref, sems.at[1]),
        pltpu.make_async_copy(pep_hbm, pep_ref, sems.at[2]),
        pltpu.make_async_copy(counts_hbm, counts_ref, sems.at[3]),
    ]
    for copy in copies:
        copy.start()
    rows, width = spectra_ref.shape
    block = 256
    gap = jnp.abs(iota((block + 2 * PAD, block), 0) - PAD - iota((block + 2 * PAD, block), 1))
    band = jnp.where((gap > 0) & (gap <= LAG), 1.0, 0.0).astype(jnp.bfloat16)
    copies[0].wait()
    rooted = jnp.sqrt(spectra_ref[...].astype(jnp.float32)).astype(jnp.bfloat16)
    padded[:, :PAD] = jnp.zeros((rows, PAD), jnp.bfloat16)
    padded[:, PAD + width :] = jnp.zeros((rows, PAD), jnp.bfloat16)
    padded[:, PAD : PAD + width] = rooted
    peak = jnp.max(rooted.astype(jnp.float32), axis=1, keepdims=True)
    scale = jnp.ones((rows, 1), jnp.float32)
    for power in (16, 8, 4, 2, 1):
        larger = scale * 2.0**power
        scale = jnp.where(peak * larger <= 256.0, larger, scale)
    copies[1].wait()
    place = iota((out_ref.shape[0], rows), 0)
    inner = place % SLOTS
    window = (place // SLOTS) * 3 + inner // 2
    named = (routes_ref[0:1, :] == window) | (routes_ref[1:2, :] == window)
    named = named & (inner < 6)
    before = jnp.where(iota((rows, rows), 0) < iota((rows, rows), 1), 1.0, 0.0)
    earlier = jnp.dot(
        jnp.where(named, 1.0, 0.0).astype(jnp.bfloat16),
        before.astype(jnp.bfloat16),
        preferred_element_type=jnp.float32,
    )
    taken = named & (earlier == (inner % 2).astype(jnp.float32))
    routing = jnp.where(taken, 1.0, 0.0).astype(jnp.bfloat16)
    leaving = []
    for start in range(0, width, block):
        background = jnp.dot(
            padded[:, start : start + block + 2 * PAD], band, preferred_element_type=jnp.float32
        )
        values = rooted[:, start : start + block].astype(jnp.float32)
        prepared = (values - background / (2.0 * LAG)).astype(jnp.bfloat16)
        prepared = (prepared.astype(jnp.float32) * scale).astype(jnp.bfloat16)
        out_ref[:, start : start + block] = jnp.dot(
            routing, prepared, preferred_element_type=jnp.float32
        ).astype(jnp.bfloat16)
        columns = pl.ds(start, block)
        leaving.append(
            pltpu.make_async_copy(
                out_ref.at[:, columns], out_hbm.at[:, columns], sems.at[5 + start // block]
            )
        )
        leaving[-1].start()
    copies[3].wait()
    mass = lax.axis_index("mass")
    windows = counts_ref.shape[0]
    named_by = routes_ref[...]
    live = jnp.zeros(named_by.shape, jnp.int32)
    for index in range(windows):
        live = jnp.where(named_by == index, counts_ref[index], live)
    where_ref[...] = jnp.zeros_like(where_ref)
    diagonal = iota((rows, rows), 0) == iota((rows, rows), 1)
    turned_scale = jnp.sum(jnp.where(diagonal, scale, 0.0), axis=0, keepdims=True)
    for pick in range(2):
        here = routes_ref[pick : pick + 1, :]
        mine = taken & (window == here)
        found = jnp.sum(jnp.where(mine, place, 0), axis=0, keepdims=True)
        lanes = slice(pick * rows, (pick + 1) * rows)
        inside = found % SLOTS
        where_ref[0:1, lanes] = ((inside // 2) * 32 + mass * 2 + inside % 2).astype(jnp.float32)
        where_ref[1:2, lanes] = (found // SLOTS).astype(jnp.float32)
        where_ref[2:3, lanes] = live[pick : pick + 1].astype(jnp.float32)
        where_ref[3:4, lanes] = turned_scale
    leaving.append(pltpu.make_async_copy(where_ref, where_hbm, sems.at[4]))
    leaving[-1].start()
    copies[2].wait()
    for step in range(pep_ref.shape[0]):
        table = pep_ref[step]
        parts = [table[:, part * 128 : part * 128 + 128] for part in range(4)]
        flat_ref[step] = jnp.concatenate(parts, axis=0).T.astype(jnp.int16)
    for copy in leaving:
        copy.wait()


def theory_of(bins, theory_ref, finished=None):
    width = bins.shape[1]
    high_place = iota((HIGH * 8, 2 * width), 0).astype(jnp.float32).astype(jnp.bfloat16)
    low_place = iota((LOW, 2 * width), 0).astype(jnp.float32).astype(jnp.bfloat16)
    one = jnp.ones((), F8)
    zero = jnp.zeros((), F8)
    member = iota((128, 128), 1) // 32 + 4 * (iota((128, 128), 0) % 2)
    low = (bins & (LOW - 1)).astype(jnp.float32).astype(jnp.bfloat16)
    high = ((bins >> 7) * 8 + member).astype(jnp.float32).astype(jnp.bfloat16)
    largest = jnp.zeros((8, 128), jnp.float32)
    for quad in range(16):
        parts = []
        for item in range(4):
            row = 8 * quad + 2 * item
            high_row = jnp.concatenate([high[row : row + 1], high[row + 1 : row + 2]], axis=1)
            low_row = jnp.concatenate([low[row : row + 1], low[row + 1 : row + 2]], axis=1)
            parts.append(
                lax.dot_general(
                    jnp.where(high_place == high_row, one, zero),
                    jnp.where(low_place == low_row, one, zero),
                    (((1,), (1,)), ((), ())),
                    preferred_element_type=jnp.float32,
                )
            )
        for part in range(HIGH):
            pieces = [item[part * 8 : part * 8 + 8] for item in parts]
            theory_ref[quad * 32 : quad * 32 + 32, part * LOW : (part + 1) * LOW] = (
                jnp.concatenate(pieces, axis=0).astype(theory_ref.dtype)
            )
            more = jnp.maximum(
                jnp.maximum(pieces[0], pieces[1]), jnp.maximum(pieces[2], pieces[3])
            )
            largest = jnp.maximum(largest, more)
        if finished is not None and quad % 4 == 3:
            finished(quad // 4)
    return largest


def theory_kernel(flat_ref, theory_ref, largest_ref):
    def window(step, carry):
        largest_ref[step] = theory_of(flat_ref[step].astype(jnp.int32), theory_ref.at[step])
        return carry

    lax.fori_loop(0, flat_ref.shape[0], window, 0)


def stored_theory_kernel(flat_ref, theory_hbm, largest_hbm, held, largest, sems):
    steps = flat_ref.shape[0]

    def copy_of(step, quarter):
        rows = pl.ds(quarter * 128, 128)
        return pltpu.make_async_copy(
            held.at[step, rows], theory_hbm.at[step, rows], sems.at[step, quarter]
        )

    def window(step, carry):
        largest[step] = theory_of(
            flat_ref[step].astype(jnp.int32),
            held.at[step],
            lambda quarter: copy_of(step, quarter).start(),
        )
        return carry

    lax.fori_loop(0, steps, window, 0)
    last = pltpu.make_async_copy(largest, largest_hbm, sems.at[steps, 0])
    last.start()
    for step in range(steps):
        for quarter in range(4):
            copy_of(step, quarter).wait()
    last.wait()


def build_theory(flat, width, stored):
    steps = flat.shape[0]
    shape, small = (steps, 512, width), (steps, 8, 128)
    space = pltpu.HBM if stored else VMEM
    scratch = [
        pltpu.VMEM(shape, F8),
        pltpu.VMEM(small, jnp.float32),
        pltpu.SemaphoreType.DMA((steps + 1, 4)),
    ]
    return pl.pallas_call(
        stored_theory_kernel if stored else theory_kernel,
        out_shape=(space(shape, F8), space(small, jnp.float32)),
        in_specs=[pl.BlockSpec(memory_space=VMEM)],
        out_specs=(pl.BlockSpec(memory_space=space),) * 2,
        scratch_shapes=scratch if stored else [],
        compiler_params=pltpu.CompilerParams(vmem_limit_bytes=(8 if stored else 4) << 20),
        cost_estimate=pl.CostEstimate(
            flops=2_000_000_000, bytes_accessed=6_400_000, transcendentals=0
        ),
        name="theory",
    )(flat)


def score_kernel(
    counts_ref,
    stored_hbm,
    stored_largest_hbm,
    theory_ref,
    largest_ref,
    flat0_ref,
    flat1_ref,
    flat2_ref,
    flat3_ref,
    own_ref,
    other_ref,
    out_ref,
    held,
    held_largest,
    built2,
    built3,
    halves,
    stats_ref,
    exact,
    exact_rows,
    tables_ref,
    sems,
):
    steps, width = theory_ref.shape[0], theory_ref.shape[2]
    flats = (flat0_ref, flat1_ref, flat2_ref, flat3_ref)

    def copy_of(step):
        return pltpu.make_async_copy(stored_hbm.at[step], held.at[step], sems.at[step])

    small = pltpu.make_async_copy(stored_largest_hbm, held_largest, sems.at[steps])
    small.start()
    for step in range(steps):
        copy_of(step).start()
    y = lax.axis_index("spec") // 2
    core = lax.axis_index("spec") % 2
    mass = lax.axis_index("mass")
    rows = own_ref.shape[0]
    local = (iota((512, 1), 0) % 4) * 128 + iota((512, 1), 0) // 4
    entry = iota((32 * steps, rows), 0)
    source = (entry % 32 // 2) * SLOTS + entry // 32 * 2 + entry % 2
    pick = jnp.where(iota((32 * steps, rows), 1) == source, 1.0, 0.0).astype(jnp.bfloat16)
    for half, ref in enumerate((own_ref, other_ref)):
        values = jnp.dot(pick, ref[...], preferred_element_type=jnp.float32)
        upper = values.astype(F8)
        lower = ((values - upper.astype(jnp.float32)) * 32.0).astype(F8)
        for step in range(steps):
            rows_now = slice(step * 32, step * 32 + 32)
            at = half * 32
            halves[step, at : at + 32, :] = upper[rows_now]
            halves[step, 64 + at : 96 + at, :] = lower[rows_now]
            exact_rows[step, at : at + 32, :] = values[rows_now].astype(jnp.bfloat16)
    small.wait()

    def reduced(scores, limit):
        valid = local < limit
        best = jnp.max(jnp.where(valid, scores, -1e30), axis=0, keepdims=True)
        scores = jnp.where(valid, scores, 0.0)
        return (
            best,
            jnp.sum(scores, axis=0, keepdims=True),
            jnp.sum(scores * scores, axis=0, keepdims=True),
        )

    def base_of(turn):
        return (lax.rem(y + turn, 4) * 2 + core) * 512

    def keep(step, found):
        stats_ref[step, 0:1, :] = functools.reduce(jnp.maximum, [item[0] for item in found])
        for row in (1, 2):
            stats_ref[step, row : row + 1, :] = functools.reduce(
                jnp.add, [item[row] for item in found]
            )

    def window(step, carry):
        live = counts_ref[mass * steps + step]
        largest = jnp.maximum(
            theory_of(flat2_ref[step].astype(jnp.int32), built2),
            theory_of(flat3_ref[step].astype(jnp.int32), built3),
        )
        largest = jnp.maximum(largest, jnp.maximum(held_largest[step], largest_ref[step]))
        beyond = jnp.max(largest) > 16.0
        copy_of(step).wait()
        found = []
        for turn, theory in enumerate((held.at[step], theory_ref.at[step], built2, built3)):
            scores = lax.dot_general(
                theory[...],
                halves[step],
                (((1,), (1,)), ((), ())),
                preferred_element_type=jnp.float32,
            )
            scores = scores + pltpu.roll(scores, 64, 1) * (1.0 / 32.0)
            found.append(reduced(scores, live - base_of(turn)))
        keep(step, found)

        @pl.when(beyond)
        def _():
            for turn in range(4):
                tables_ref[turn] = flats[turn][step].astype(jnp.int32)
            values = exact_rows[step]
            values = jnp.concatenate([values, jnp.zeros_like(values)], axis=0)

            def piece(turn, found):
                theory_of(tables_ref[turn], exact)
                scores = lax.dot_general(
                    exact[...],
                    values,
                    (((1,), (1,)), ((), ())),
                    preferred_element_type=jnp.float32,
                )
                more = reduced(scores, live - base_of(turn))
                return (
                    jnp.maximum(found[0], more[0]),
                    found[1] + more[1],
                    found[2] + more[2],
                )

            zeros = jnp.zeros((1, 128), jnp.float32)
            keep(step, [lax.fori_loop(0, 4, piece, (zeros - 1e30, zeros, zeros))])

        return carry

    stats_ref[...] = jnp.zeros_like(stats_ref)
    lax.fori_loop(0, steps, window, 0)
    part = iota((8, 128), 1) // 32
    tiles = []
    for half in range(2):
        tile = jnp.zeros((8, 128), jnp.float32)
        for step in range(steps):
            moved = pltpu.roll(stats_ref[step], (step * 32 - half * 32) % 128, 1)
            tile = jnp.where(part == step, moved, tile)
        tiles.append(tile)
    first = jnp.where(core == 0, tiles[0], tiles[1])
    second = jnp.where(core == 0, tiles[1], tiles[0])
    peers = out_ref.shape[0] // 16
    for peer in range(peers):
        out_ref[peer * 8 : peer * 8 + 8, :] = first
        out_ref[(peers + peer) * 8 : (peers + peer) * 8 + 8, :] = second


def finish_kernel(where_hbm, stats_hbm, best_ref, z_ref, where_ref, stats_ref, sems):
    copies = [
        pltpu.make_async_copy(stats_hbm, stats_ref, sems.at[0]),
        pltpu.make_async_copy(where_hbm, where_ref, sems.at[1]),
    ]
    for copy in copies:
        copy.start()
    for copy in copies:
        copy.wait()
    rows = best_ref.shape[1]
    peers = stats_ref.shape[0] // 16
    lane = jnp.broadcast_to(where_ref[0:1, :].astype(jnp.int32), (8, 128))
    shard = where_ref[1:2, :].astype(jnp.int32)
    live = where_ref[2:3, :]
    unscale = 1.0 / (where_ref[3:4, :] * 32.0)
    halves = []
    for half in range(2):
        chosen = jnp.zeros((8, 128), jnp.float32)
        for peer in range(peers):
            at = (half * peers + peer) * 8
            found = jnp.take_along_axis(stats_ref[at : at + 8, :], lane, axis=1)
            chosen = jnp.where(shard == peer, found, chosen)
        halves.append(chosen)
    best = jnp.maximum(halves[0][0:1], halves[1][0:1]) * unscale
    total = (halves[0][1:2] + halves[1][1:2]) * unscale
    square = (halves[0][2:3] + halves[1][2:3]) * unscale * unscale
    mean = total / live
    spread = square / live - mean * mean
    z = (best - mean) / jnp.sqrt(spread + EPS)
    best_ref[0:1, :] = best[:, :rows]
    best_ref[1:2, :] = best[:, rows : 2 * rows]
    z_ref[0:1, :] = z[:, :rows]
    z_ref[1:2, :] = z[:, rows : 2 * rows]


def per_device(spectra, routes, pep_bins, counts):
    rows, width = spectra.shape
    mass_count = lax.axis_size("mass")
    spec_count = lax.axis_size("spec")
    steps = pep_bins.shape[0]
    routes_t = routes.T
    vmem = pl.BlockSpec(memory_space=VMEM)
    smem = pl.BlockSpec(memory_space=SMEM)
    hbm = pl.BlockSpec(memory_space=pltpu.HBM)
    outgoing, flat, where = pl.pallas_call(
        prepare_kernel,
        out_shape=(
            pltpu.HBM((mass_count * SLOTS, width), jnp.bfloat16),
            jax.ShapeDtypeStruct((steps, 128, 128), jnp.int16),
            pltpu.HBM((8, 128), jnp.float32),
        ),
        in_specs=[hbm] * 4,
        out_specs=(hbm, vmem, hbm),
        scratch_shapes=[
            pltpu.VMEM((mass_count * SLOTS, width), jnp.bfloat16),
            pltpu.VMEM((8, 128), jnp.float32),
            pltpu.SMEM(counts.shape, counts.dtype),
            pltpu.VMEM((rows, width), spectra.dtype),
            pltpu.VMEM(routes_t.shape, routes_t.dtype),
            pltpu.VMEM(pep_bins.shape, pep_bins.dtype),
            pltpu.VMEM((rows, width + 2 * PAD), jnp.bfloat16),
            pltpu.SemaphoreType.DMA((5 + width // 256,)),
        ],
        compiler_params=pltpu.CompilerParams(vmem_limit_bytes=8 << 20),
        name="prepare",
    )(
        *[
            pltpu.with_memory_space_constraint(item, pltpu.HBM)
            for item in (spectra, routes_t, pep_bins, counts)
        ]
    )
    flats = [flat] + [
        lax.ppermute(
            flat, "spec", [((i + 2 * turn) % spec_count, i) for i in range(spec_count)]
        )
        for turn in range(1, 4)
    ]
    own = lax.all_to_all(outgoing, "mass", split_axis=0, concat_axis=0, tiled=True)
    first, first_largest = build_theory(flats[0], width, True)
    own, first, flats = lax.optimization_barrier((own, first, flats))
    other = lax.ppermute(own, "spec", [(i, i ^ 1) for i in range(spec_count)])
    second, second_largest = build_theory(flats[1], width, False)
    stats = pl.pallas_call(
        score_kernel,
        out_shape=jax.ShapeDtypeStruct((2 * mass_count * 8, 128), jnp.float32),
        in_specs=[smem, hbm, hbm] + [vmem] * 8,
        out_specs=vmem,
        scratch_shapes=[
            pltpu.VMEM((steps, 512, width), F8),
            pltpu.VMEM((steps, 8, 128), jnp.float32),
            pltpu.VMEM((512, width), F8),
            pltpu.VMEM((512, width), F8),
            pltpu.VMEM((steps, 128, width), F8),
            pltpu.VMEM((steps, 8, 128), jnp.float32),
            pltpu.VMEM((512, width), jnp.bfloat16),
            pltpu.VMEM((steps, 64, width), jnp.bfloat16),
            pltpu.VMEM((4, 128, 128), jnp.int32),
            pltpu.SemaphoreType.DMA((steps + 1,)),
        ],
        compiler_params=pltpu.CompilerParams(vmem_limit_bytes=24 << 20),
        name="score",
    )(
        counts,
        pltpu.with_memory_space_constraint(first, pltpu.HBM),
        pltpu.with_memory_space_constraint(first_largest, pltpu.HBM),
        second,
        second_largest,
        *flats,
        own,
        other,
    )
    groups = [
        [(y * 2 + core) * mass_count + m for core in range(2) for m in range(mass_count)]
        for y in range(spec_count // 2)
    ]
    back = lax.all_to_all(
        stats,
        ("spec", "mass"),
        split_axis=0,
        concat_axis=0,
        tiled=True,
        axis_index_groups=groups,
    )
    best, z = pl.pallas_call(
        finish_kernel,
        out_shape=(jax.ShapeDtypeStruct((2, rows), jnp.float32),) * 2,
        in_specs=[hbm] * 2,
        out_specs=(vmem, vmem),
        scratch_shapes=[
            pltpu.VMEM((8, 128), jnp.float32),
            pltpu.VMEM(back.shape, jnp.float32),
            pltpu.SemaphoreType.DMA((2,)),
        ],
        name="finish",
    )(*[pltpu.with_memory_space_constraint(item, pltpu.HBM) for item in (where, back)])
    return best.T, z.T


def solution(mesh):
    return jax.shard_map(
        per_device,
        mesh=mesh,
        in_specs=(
            P(("spec", "mass"), None),
            P(("spec", "mass"), None),
            P("mass", None, "spec"),
            P(),
        ),
        out_specs=(P(("spec", "mass"), None), P(("spec", "mass"), None)),
        check_vma=False,
    )
```

```python
import functools

import jax
import jax.numpy as jnp
from jax import lax
from jax.experimental import pallas as pl
from jax.experimental.pallas import tpu as pltpu
from jax.sharding import PartitionSpec as P

LAG = 75
EPS = 1e-06
PAD = 128
SLOTS = 8
LOW = 128
HIGH = 16
F8 = jnp.float8_e4m3fn
VMEM = pltpu.VMEM
SMEM = pltpu.SMEM


def iota(shape, axis):
    return lax.broadcasted_iota(jnp.int32, shape, axis)


def prepare_kernel(
    spectra_hbm,
    routes_hbm,
    pep_hbm,
    counts_hbm,
    out_hbm,
    flat_ref,
    where_hbm,
    out_ref,
    where_ref,
    counts_ref,
    spectra_ref,
    routes_ref,
    pep_ref,
    padded,
    sems,
):
    copies = [
        pltpu.make_async_copy(spectra_hbm, spectra_ref, sems.at[0]),
        pltpu.make_async_copy(routes_hbm, routes_ref, sems.at[1]),
        pltpu.make_async_copy(pep_hbm, pep_ref, sems.at[2]),
        pltpu.make_async_copy(counts_hbm, counts_ref, sems.at[3]),
    ]
    for copy in copies:
        copy.start()
    rows, width = spectra_ref.shape
    block = 256
    gap = jnp.abs(iota((block + 2 * PAD, block), 0) - PAD - iota((block + 2 * PAD, block), 1))
    band = jnp.where((gap > 0) & (gap <= LAG), 1.0, 0.0).astype(jnp.bfloat16)
    copies[0].wait()
    rooted = jnp.sqrt(spectra_ref[...].astype(jnp.float32)).astype(jnp.bfloat16)
    padded[:, :PAD] = jnp.zeros((rows, PAD), jnp.bfloat16)
    padded[:, PAD + width :] = jnp.zeros((rows, PAD), jnp.bfloat16)
    padded[:, PAD : PAD + width] = rooted
    peak = jnp.max(rooted.astype(jnp.float32), axis=1, keepdims=True)
    scale = jnp.ones((rows, 1), jnp.float32)
    for power in (16, 8, 4, 2, 1):
        larger = scale * 2.0**power
        scale = jnp.where(peak * larger <= 256.0, larger, scale)
    copies[1].wait()
    place = iota((out_ref.shape[0], rows), 0)
    inner = place % SLOTS
    window = (place // SLOTS) * 3 + inner // 2
    named = (routes_ref[0:1, :] == window) | (routes_ref[1:2, :] == window)
    named = named & (inner < 6)
    before = jnp.where(iota((rows, rows), 0) < iota((rows, rows), 1), 1.0, 0.0)
    earlier = jnp.dot(
        jnp.where(named, 1.0, 0.0).astype(jnp.bfloat16),
        before.astype(jnp.bfloat16),
        preferred_element_type=jnp.float32,
    )
    taken = named & (earlier == (inner % 2).astype(jnp.float32))
    routing = jnp.where(taken, 1.0, 0.0).astype(jnp.bfloat16)
    blocks = [padded[:, start : start + block + 2 * PAD] for start in range(0, width, block)]
    background = jnp.dot(
        jnp.concatenate(blocks, axis=0), band, preferred_element_type=jnp.float32
    )
    leaving = []
    for start in range(0, width, block):
        at = start // block * rows
        values = rooted[:, start : start + block].astype(jnp.float32)
        prepared = values - background[at : at + rows] / (2.0 * LAG)
        prepared = prepared.astype(jnp.bfloat16)
        prepared = (prepared.astype(jnp.float32) * scale).astype(jnp.bfloat16)
        out_ref[:, start : start + block] = jnp.dot(
            routing, prepared, preferred_element_type=jnp.float32
        ).astype(jnp.bfloat16)
        columns = pl.ds(start, block)
        leaving.append(
            pltpu.make_async_copy(
                out_ref.at[:, columns], out_hbm.at[:, columns], sems.at[5 + start // block]
            )
        )
        leaving[-1].start()
    copies[3].wait()
    mass = lax.axis_index("mass")
    windows = counts_ref.shape[0]
    named_by = routes_ref[...]
    live = jnp.zeros(named_by.shape, jnp.int32)
    for index in range(windows):
        live = jnp.where(named_by == index, counts_ref[index], live)
    where_ref[...] = jnp.zeros_like(where_ref)
    diagonal = iota((rows, rows), 0) == iota((rows, rows), 1)
    turned_scale = jnp.sum(jnp.where(diagonal, scale, 0.0), axis=0, keepdims=True)
    for pick in range(2):
        here = routes_ref[pick : pick + 1, :]
        mine = taken & (window == here)
        found = jnp.sum(jnp.where(mine, place, 0), axis=0, keepdims=True)
        lanes = slice(pick * rows, (pick + 1) * rows)
        inside = found % SLOTS
        where_ref[0:1, lanes] = ((inside // 2) * 32 + mass * 2 + inside % 2).astype(jnp.float32)
        where_ref[1:2, lanes] = (found // SLOTS).astype(jnp.float32)
        where_ref[2:3, lanes] = live[pick : pick + 1].astype(jnp.float32)
        where_ref[3:4, lanes] = turned_scale
    leaving.append(pltpu.make_async_copy(where_ref, where_hbm, sems.at[4]))
    leaving[-1].start()
    copies[2].wait()
    for step in range(pep_ref.shape[0]):
        table = pep_ref[step]
        parts = [table[:, part * 128 : part * 128 + 128] for part in range(4)]
        flat_ref[step] = jnp.concatenate(parts, axis=0).T.astype(jnp.int16)
    for copy in leaving:
        copy.wait()


def theory_of(bins, theory_ref, finished=None):
    width = bins.shape[1]
    high_place = iota((HIGH * 8, 2 * width), 0).astype(jnp.float32).astype(jnp.bfloat16)
    low_place = iota((LOW, 2 * width), 0).astype(jnp.float32).astype(jnp.bfloat16)
    one = jnp.ones((), F8)
    zero = jnp.zeros((), F8)
    member = iota((128, 128), 1) // 32 + 4 * (iota((128, 128), 0) % 2)
    low = (bins & (LOW - 1)).astype(jnp.float32).astype(jnp.bfloat16)
    high = ((bins >> 7) * 8 + member).astype(jnp.float32).astype(jnp.bfloat16)
    largest = jnp.zeros((8, 128), jnp.float32)
    for quad in range(16):
        parts = []
        for item in range(4):
            row = 8 * quad + 2 * item
            high_row = jnp.concatenate([high[row : row + 1], high[row + 1 : row + 2]], axis=1)
            low_row = jnp.concatenate([low[row : row + 1], low[row + 1 : row + 2]], axis=1)
            parts.append(
                lax.dot_general(
                    jnp.where(high_place == high_row, one, zero),
                    jnp.where(low_place == low_row, one, zero),
                    (((1,), (1,)), ((), ())),
                    preferred_element_type=jnp.float32,
                )
            )
        for part in range(HIGH):
            pieces = [item[part * 8 : part * 8 + 8] for item in parts]
            theory_ref[quad * 32 : quad * 32 + 32, part * LOW : (part + 1) * LOW] = (
                jnp.concatenate(pieces, axis=0).astype(theory_ref.dtype)
            )
            more = jnp.maximum(
                jnp.maximum(pieces[0], pieces[1]), jnp.maximum(pieces[2], pieces[3])
            )
            largest = jnp.maximum(largest, more)
        if finished is not None and quad % 4 == 3:
            finished(quad // 4)
    return largest


def theory_kernel(flat_ref, theory_ref, largest_ref):
    def window(step, carry):
        largest_ref[step] = theory_of(flat_ref[step].astype(jnp.int32), theory_ref.at[step])
        return carry

    lax.fori_loop(0, flat_ref.shape[0], window, 0)


def stored_theory_kernel(flat_ref, theory_hbm, largest_hbm, held, largest, sems):
    steps = flat_ref.shape[0]

    def copy_of(step, quarter):
        rows = pl.ds(quarter * 128, 128)
        return pltpu.make_async_copy(
            held.at[step, rows], theory_hbm.at[step, rows], sems.at[step, quarter]
        )

    def window(step, carry):
        largest[step] = theory_of(
            flat_ref[step].astype(jnp.int32),
            held.at[step],
            lambda quarter: copy_of(step, quarter).start(),
        )
        return carry

    lax.fori_loop(0, steps, window, 0)
    last = pltpu.make_async_copy(largest, largest_hbm, sems.at[steps, 0])
    last.start()
    for step in range(steps):
        for quarter in range(4):
            copy_of(step, quarter).wait()
    last.wait()


def build_theory(flat, width, stored):
    steps = flat.shape[0]
    shape, small = (steps, 512, width), (steps, 8, 128)
    space = pltpu.HBM if stored else VMEM
    scratch = [
        pltpu.VMEM(shape, F8),
        pltpu.VMEM(small, jnp.float32),
        pltpu.SemaphoreType.DMA((steps + 1, 4)),
    ]
    return pl.pallas_call(
        stored_theory_kernel if stored else theory_kernel,
        out_shape=(space(shape, F8), space(small, jnp.float32)),
        in_specs=[pl.BlockSpec(memory_space=VMEM)],
        out_specs=(pl.BlockSpec(memory_space=space),) * 2,
        scratch_shapes=scratch if stored else [],
        compiler_params=pltpu.CompilerParams(vmem_limit_bytes=(8 if stored else 4) << 20),
        cost_estimate=pl.CostEstimate(
            flops=2_000_000_000, bytes_accessed=6_400_000, transcendentals=0
        ),
        name="theory",
    )(flat)


def score_kernel(
    counts_ref,
    stored_hbm,
    stored_largest_hbm,
    theory_ref,
    largest_ref,
    flat0_ref,
    flat1_ref,
    flat2_ref,
    flat3_ref,
    own_ref,
    other_ref,
    out_ref,
    held,
    held_largest,
    built2,
    built3,
    halves,
    stats_ref,
    exact,
    tables_ref,
    sems,
):
    steps, width = theory_ref.shape[0], theory_ref.shape[2]
    flats = (flat0_ref, flat1_ref, flat2_ref, flat3_ref)

    def copy_of(step):
        return pltpu.make_async_copy(stored_hbm.at[step], held.at[step], sems.at[step])

    small = pltpu.make_async_copy(stored_largest_hbm, held_largest, sems.at[steps])
    small.start()
    for step in range(steps):
        copy_of(step).start()
    y = lax.axis_index("spec") // 2
    core = lax.axis_index("spec") % 2
    mass = lax.axis_index("mass")
    rows = own_ref.shape[0]
    local = (iota((512, 1), 0) % 4) * 128 + iota((512, 1), 0) // 4
    entry = iota((32 * steps, rows), 0)
    source = (entry % 32 // 2) * SLOTS + entry // 32 * 2 + entry % 2
    pick = jnp.where(iota((32 * steps, rows), 1) == source, 1.0, 0.0).astype(jnp.bfloat16)
    for half, ref in enumerate((own_ref, other_ref)):
        values = jnp.dot(pick, ref[...], preferred_element_type=jnp.float32)
        upper = values.astype(F8)
        lower = ((values - upper.astype(jnp.float32)) * 32.0).astype(F8)
        for step in range(steps):
            rows_now = slice(step * 32, step * 32 + 32)
            at = half * 32
            halves[step, at : at + 32, :] = upper[rows_now]
            halves[step, 64 + at : 96 + at, :] = lower[rows_now]
    small.wait()

    def reduced(scores, limit):
        valid = local < limit
        best = jnp.max(jnp.where(valid, scores, -1e30), axis=0, keepdims=True)
        scores = jnp.where(valid, scores, 0.0)
        return (
            best,
            jnp.sum(scores, axis=0, keepdims=True),
            jnp.sum(scores * scores, axis=0, keepdims=True),
        )

    def base_of(turn):
        return (lax.rem(y + turn, 4) * 2 + core) * 512

    def keep(step, found):
        stats_ref[step, 0:1, :] = functools.reduce(jnp.maximum, [item[0] for item in found])
        for row in (1, 2):
            stats_ref[step, row : row + 1, :] = functools.reduce(
                jnp.add, [item[row] for item in found]
            )

    def window(step, largest):
        live = counts_ref[mass * steps + step]
        largest = jnp.maximum(largest, theory_of(flat2_ref[step].astype(jnp.int32), built2))
        largest = jnp.maximum(largest, theory_of(flat3_ref[step].astype(jnp.int32), built3))
        largest = jnp.maximum(largest, jnp.maximum(held_largest[step], largest_ref[step]))
        copy_of(step).wait()
        found = []
        for turn, theory in enumerate((held.at[step], theory_ref.at[step], built2, built3)):
            scores = lax.dot_general(
                theory[...],
                halves[step],
                (((1,), (1,)), ((), ())),
                preferred_element_type=jnp.float32,
            )
            scores = scores + pltpu.roll(scores, 64, 1) * (1.0 / 32.0)
            found.append(reduced(scores, live - base_of(turn)))
        keep(step, found)
        return largest

    def exact_window(step, carry):
        live = counts_ref[mass * steps + step]
        for turn in range(4):
            tables_ref[turn] = flats[turn][step].astype(jnp.int32)
        own_entry = iota((64, rows), 0)
        mine = (own_entry % 32 // 2) * SLOTS + step * 2 + own_entry % 2
        mine = iota((64, rows), 1) == mine
        values = sum(
            jnp.dot(
                jnp.where(mine & (own_entry // 32 == half), 1.0, 0.0).astype(jnp.bfloat16),
                ref[...],
                preferred_element_type=jnp.float32,
            )
            for half, ref in enumerate((own_ref, other_ref))
        ).astype(jnp.bfloat16)
        values = jnp.concatenate([values, jnp.zeros_like(values)], axis=0)

        def piece(turn, found):
            theory_of(tables_ref[turn], exact)
            scores = lax.dot_general(
                exact[...],
                values,
                (((1,), (1,)), ((), ())),
                preferred_element_type=jnp.float32,
            )
            more = reduced(scores, live - base_of(turn))
            return (
                jnp.maximum(found[0], more[0]),
                found[1] + more[1],
                found[2] + more[2],
            )

        zeros = jnp.zeros((1, 128), jnp.float32)
        keep(step, [lax.fori_loop(0, 4, piece, (zeros - 1e30, zeros, zeros))])
        return carry

    stats_ref[...] = jnp.zeros_like(stats_ref)
    largest = lax.fori_loop(0, steps, window, jnp.zeros((8, 128), jnp.float32))

    @pl.when(jnp.max(largest) > 16.0)
    def _():
        lax.fori_loop(0, steps, exact_window, 0)

    part = iota((8, 128), 1) // 32
    tiles = []
    for half in range(2):
        tile = jnp.zeros((8, 128), jnp.float32)
        for step in range(steps):
            moved = pltpu.roll(stats_ref[step], (step * 32 - half * 32) % 128, 1)
            tile = jnp.where(part == step, moved, tile)
        tiles.append(tile)
    first = jnp.where(core == 0, tiles[0], tiles[1])
    second = jnp.where(core == 0, tiles[1], tiles[0])
    peers = out_ref.shape[0] // 16
    for peer in range(peers):
        out_ref[peer * 8 : peer * 8 + 8, :] = first
        out_ref[(peers + peer) * 8 : (peers + peer) * 8 + 8, :] = second


def finish_kernel(where_hbm, stats_hbm, best_ref, z_ref, where_ref, stats_ref, sems):
    copies = [
        pltpu.make_async_copy(stats_hbm, stats_ref, sems.at[0]),
        pltpu.make_async_copy(where_hbm, where_ref, sems.at[1]),
    ]
    for copy in copies:
        copy.start()
    for copy in copies:
        copy.wait()
    rows = best_ref.shape[1]
    peers = stats_ref.shape[0] // 16
    lane = jnp.broadcast_to(where_ref[0:1, :].astype(jnp.int32), (8, 128))
    shard = where_ref[1:2, :].astype(jnp.int32)
    live = where_ref[2:3, :]
    unscale = 1.0 / (where_ref[3:4, :] * 32.0)
    halves = []
    for half in range(2):
        chosen = jnp.zeros((8, 128), jnp.float32)
        for peer in range(peers):
            at = (half * peers + peer) * 8
            found = jnp.take_along_axis(stats_ref[at : at + 8, :], lane, axis=1)
            chosen = jnp.where(shard == peer, found, chosen)
        halves.append(chosen)
    best = jnp.maximum(halves[0][0:1], halves[1][0:1]) * unscale
    total = (halves[0][1:2] + halves[1][1:2]) * unscale
    square = (halves[0][2:3] + halves[1][2:3]) * unscale * unscale
    mean = total / live
    spread = square / live - mean * mean
    z = (best - mean) / jnp.sqrt(spread + EPS)
    best_ref[0:1, :] = best[:, :rows]
    best_ref[1:2, :] = best[:, rows : 2 * rows]
    z_ref[0:1, :] = z[:, :rows]
    z_ref[1:2, :] = z[:, rows : 2 * rows]


def per_device(spectra, routes, pep_bins, counts):
    rows, width = spectra.shape
    mass_count = lax.axis_size("mass")
    spec_count = lax.axis_size("spec")
    steps = pep_bins.shape[0]
    routes_t = routes.T
    vmem = pl.BlockSpec(memory_space=VMEM)
    smem = pl.BlockSpec(memory_space=SMEM)
    hbm = pl.BlockSpec(memory_space=pltpu.HBM)
    outgoing, flat, where = pl.pallas_call(
        prepare_kernel,
        out_shape=(
            pltpu.HBM((mass_count * SLOTS, width), jnp.bfloat16),
            jax.ShapeDtypeStruct((steps, 128, 128), jnp.int16),
            pltpu.HBM((8, 128), jnp.float32),
        ),
        in_specs=[hbm] * 4,
        out_specs=(hbm, vmem, hbm),
        scratch_shapes=[
            pltpu.VMEM((mass_count * SLOTS, width), jnp.bfloat16),
            pltpu.VMEM((8, 128), jnp.float32),
            pltpu.SMEM(counts.shape, counts.dtype),
            pltpu.VMEM((rows, width), spectra.dtype),
            pltpu.VMEM(routes_t.shape, routes_t.dtype),
            pltpu.VMEM(pep_bins.shape, pep_bins.dtype),
            pltpu.VMEM((rows, width + 2 * PAD), jnp.bfloat16),
            pltpu.SemaphoreType.DMA((5 + width // 256,)),
        ],
        compiler_params=pltpu.CompilerParams(vmem_limit_bytes=8 << 20),
        name="prepare",
    )(
        *[
            pltpu.with_memory_space_constraint(item, pltpu.HBM)
            for item in (spectra, routes_t, pep_bins, counts)
        ]
    )
    flats = [flat] + [
        lax.ppermute(
            flat, "spec", [((i + 2 * turn) % spec_count, i) for i in range(spec_count)]
        )
        for turn in range(1, 4)
    ]
    own = lax.all_to_all(outgoing, "mass", split_axis=0, concat_axis=0, tiled=True)
    first, first_largest = build_theory(flats[0], width, True)
    own, first, flats = lax.optimization_barrier((own, first, flats))
    other = lax.ppermute(own, "spec", [(i, i ^ 1) for i in range(spec_count)])
    second, second_largest = build_theory(flats[1], width, False)
    stats = pl.pallas_call(
        score_kernel,
        out_shape=jax.ShapeDtypeStruct((2 * mass_count * 8, 128), jnp.float32),
        in_specs=[smem, hbm, hbm] + [vmem] * 8,
        out_specs=vmem,
        scratch_shapes=[
            pltpu.VMEM((steps, 512, width), F8),
            pltpu.VMEM((steps, 8, 128), jnp.float32),
            pltpu.VMEM((512, width), F8),
            pltpu.VMEM((512, width), F8),
            pltpu.VMEM((steps, 128, width), F8),
            pltpu.VMEM((steps, 8, 128), jnp.float32),
            pltpu.VMEM((512, width), jnp.bfloat16),
            pltpu.VMEM((4, 128, 128), jnp.int32),
            pltpu.SemaphoreType.DMA((steps + 1,)),
        ],
        compiler_params=pltpu.CompilerParams(vmem_limit_bytes=24 << 20),
        name="score",
    )(
        counts,
        pltpu.with_memory_space_constraint(first, pltpu.HBM),
        pltpu.with_memory_space_constraint(first_largest, pltpu.HBM),
        second,
        second_largest,
        *flats,
        own,
        other,
    )
    groups = [
        [(y * 2 + core) * mass_count + m for core in range(2) for m in range(mass_count)]
        for y in range(spec_count // 2)
    ]
    back = lax.all_to_all(
        stats,
        ("spec", "mass"),
        split_axis=0,
        concat_axis=0,
        tiled=True,
        axis_index_groups=groups,
    )
    best, z = pl.pallas_call(
        finish_kernel,
        out_shape=(jax.ShapeDtypeStruct((2, rows), jnp.float32),) * 2,
        in_specs=[hbm] * 2,
        out_specs=(vmem, vmem),
        scratch_shapes=[
            pltpu.VMEM((8, 128), jnp.float32),
            pltpu.VMEM(back.shape, jnp.float32),
            pltpu.SemaphoreType.DMA((2,)),
        ],
        name="finish",
    )(*[pltpu.with_memory_space_constraint(item, pltpu.HBM) for item in (where, back)])
    return best.T, z.T


def solution(mesh):
    return jax.shard_map(
        per_device,
        mesh=mesh,
        in_specs=(
            P(("spec", "mass"), None),
            P(("spec", "mass"), None),
            P("mass", None, "spec"),
            P(),
        ),
        out_specs=(P(("spec", "mass"), None), P(("spec", "mass"), None)),
        check_vma=False,
    )
```

```python
import functools

import jax
import jax.numpy as jnp
from jax import lax
from jax.experimental import pallas as pl
from jax.experimental.pallas import tpu as pltpu
from jax.sharding import PartitionSpec as P

LAG = 75
EPS = 1e-06
PAD = 128
SLOTS = 8
LOW = 128
HIGH = 16
F8 = jnp.float8_e4m3fn
VMEM = pltpu.VMEM
SMEM = pltpu.SMEM


def iota(shape, axis):
    return lax.broadcasted_iota(jnp.int32, shape, axis)


def prepare_kernel(
    spectra_hbm,
    routes_hbm,
    pep_hbm,
    counts_hbm,
    out_hbm,
    flat_ref,
    where_hbm,
    out_ref,
    where_ref,
    counts_ref,
    spectra_ref,
    routes_ref,
    pep_ref,
    padded,
    sems,
):
    copies = [
        pltpu.make_async_copy(spectra_hbm, spectra_ref, sems.at[0]),
        pltpu.make_async_copy(routes_hbm, routes_ref, sems.at[1]),
        pltpu.make_async_copy(pep_hbm, pep_ref, sems.at[2]),
        pltpu.make_async_copy(counts_hbm, counts_ref, sems.at[3]),
    ]
    for copy in copies:
        copy.start()
    rows, width = spectra_ref.shape
    block = 256
    gap = jnp.abs(iota((block + 2 * PAD, block), 0) - PAD - iota((block + 2 * PAD, block), 1))
    band = jnp.where((gap > 0) & (gap <= LAG), 1.0, 0.0).astype(jnp.bfloat16)
    copies[0].wait()
    rooted = jnp.sqrt(spectra_ref[...].astype(jnp.float32)).astype(jnp.bfloat16)
    padded[:, :PAD] = jnp.zeros((rows, PAD), jnp.bfloat16)
    padded[:, PAD + width :] = jnp.zeros((rows, PAD), jnp.bfloat16)
    padded[:, PAD : PAD + width] = rooted
    peak = jnp.max(rooted.astype(jnp.float32), axis=1, keepdims=True)
    scale = jnp.ones((rows, 1), jnp.float32)
    for power in (16, 8, 4, 2, 1):
        larger = scale * 2.0**power
        scale = jnp.where(peak * larger <= 256.0, larger, scale)
    copies[1].wait()
    place = iota((out_ref.shape[0], rows), 0)
    inner = place % SLOTS
    window = (place // SLOTS) * 3 + inner // 2
    named = (routes_ref[0:1, :] == window) | (routes_ref[1:2, :] == window)
    named = named & (inner < 6)
    before = jnp.where(iota((rows, rows), 0) < iota((rows, rows), 1), 1.0, 0.0)
    earlier = jnp.dot(
        jnp.where(named, 1.0, 0.0).astype(jnp.bfloat16),
        before.astype(jnp.bfloat16),
        preferred_element_type=jnp.float32,
    )
    taken = named & (earlier == (inner % 2).astype(jnp.float32))
    routing = jnp.where(taken, 1.0, 0.0).astype(jnp.bfloat16)
    blocks = [padded[:, start : start + block + 2 * PAD] for start in range(0, width, block)]
    background = jnp.dot(
        jnp.concatenate(blocks, axis=0), band, preferred_element_type=jnp.float32
    )
    leaving = []
    for start in range(0, width, block):
        at = start // block * rows
        values = rooted[:, start : start + block].astype(jnp.float32)
        prepared = values - background[at : at + rows] / (2.0 * LAG)
        prepared = prepared.astype(jnp.bfloat16)
        prepared = (prepared.astype(jnp.float32) * scale).astype(jnp.bfloat16)
        out_ref[:, start : start + block] = jnp.dot(
            routing, prepared, preferred_element_type=jnp.float32
        ).astype(jnp.bfloat16)
        columns = pl.ds(start, block)
        leaving.append(
            pltpu.make_async_copy(
                out_ref.at[:, columns], out_hbm.at[:, columns], sems.at[5 + start // block]
            )
        )
        leaving[-1].start()
    copies[3].wait()
    windows = counts_ref.shape[0]
    named_by = routes_ref[...]
    live = jnp.zeros(named_by.shape, jnp.int32)
    for index in range(windows):
        live = jnp.where(named_by == index, counts_ref[index], live)
    where_ref[...] = jnp.zeros_like(where_ref)
    diagonal = iota((rows, rows), 0) == iota((rows, rows), 1)
    turned_scale = jnp.sum(jnp.where(diagonal, scale, 0.0), axis=0, keepdims=True)
    for pick in range(2):
        here = routes_ref[pick : pick + 1, :]
        mine = taken & (window == here)
        found = jnp.sum(jnp.where(mine, place, 0), axis=0, keepdims=True)
        lanes = slice(pick * rows, (pick + 1) * rows)
        inside = found % SLOTS
        where_ref[0:1, lanes] = ((inside // 2) * 32 + inside % 2).astype(jnp.float32)
        where_ref[1:2, lanes] = (found // SLOTS).astype(jnp.float32)
        where_ref[2:3, lanes] = live[pick : pick + 1].astype(jnp.float32)
        where_ref[3:4, lanes] = turned_scale
    leaving.append(pltpu.make_async_copy(where_ref, where_hbm, sems.at[4]))
    leaving[-1].start()
    copies[2].wait()
    for step in range(pep_ref.shape[0]):
        table = pep_ref[step]
        parts = [table[:, part * 128 : part * 128 + 128] for part in range(4)]
        flat_ref[step] = jnp.concatenate(parts, axis=0).T.astype(jnp.int16)
    for copy in leaving:
        copy.wait()


def theory_of(bins, theory_ref, finished=None):
    width = bins.shape[1]
    high_place = iota((HIGH * 8, 2 * width), 0).astype(jnp.float32).astype(jnp.bfloat16)
    low_place = iota((LOW, 2 * width), 0).astype(jnp.float32).astype(jnp.bfloat16)
    one = jnp.ones((), F8)
    zero = jnp.zeros((), F8)
    member = iota((128, 128), 1) // 32 + 4 * (iota((128, 128), 0) % 2)
    low = (bins & (LOW - 1)).astype(jnp.float32).astype(jnp.bfloat16)
    high = ((bins >> 7) * 8 + member).astype(jnp.float32).astype(jnp.bfloat16)
    largest = jnp.zeros((8, 128), jnp.float32)
    for quad in range(16):
        parts = []
        for item in range(4):
            row = 8 * quad + 2 * item
            high_row = jnp.concatenate([high[row : row + 1], high[row + 1 : row + 2]], axis=1)
            low_row = jnp.concatenate([low[row : row + 1], low[row + 1 : row + 2]], axis=1)
            parts.append(
                lax.dot_general(
                    jnp.where(high_place == high_row, one, zero),
                    jnp.where(low_place == low_row, one, zero),
                    (((1,), (1,)), ((), ())),
                    preferred_element_type=jnp.float32,
                )
            )
        for part in range(HIGH):
            pieces = [item[part * 8 : part * 8 + 8] for item in parts]
            theory_ref[quad * 32 : quad * 32 + 32, part * LOW : (part + 1) * LOW] = (
                jnp.concatenate(pieces, axis=0).astype(theory_ref.dtype)
            )
            more = jnp.maximum(
                jnp.maximum(pieces[0], pieces[1]), jnp.maximum(pieces[2], pieces[3])
            )
            largest = jnp.maximum(largest, more)
        if finished is not None and quad % 4 == 3:
            finished(quad // 4)
    return largest


def theory_kernel(flat_ref, theory_ref, largest_ref):
    def window(step, carry):
        largest_ref[step] = theory_of(flat_ref[step].astype(jnp.int32), theory_ref.at[step])
        return carry

    lax.fori_loop(0, flat_ref.shape[0], window, 0)


def stored_theory_kernel(flat_ref, theory_hbm, largest_hbm, held, largest, sems):
    steps = flat_ref.shape[0]

    def copy_of(step, quarter):
        rows = pl.ds(quarter * 128, 128)
        return pltpu.make_async_copy(
            held.at[step, rows], theory_hbm.at[step, rows], sems.at[step, quarter]
        )

    def window(step, carry):
        largest[step] = theory_of(
            flat_ref[step].astype(jnp.int32),
            held.at[step],
            lambda quarter: copy_of(step, quarter).start(),
        )
        return carry

    lax.fori_loop(0, steps, window, 0)
    last = pltpu.make_async_copy(largest, largest_hbm, sems.at[steps, 0])
    last.start()
    for step in range(steps):
        for quarter in range(4):
            copy_of(step, quarter).wait()
    last.wait()


def build_theory(flat, width, stored):
    steps = flat.shape[0]
    shape, small = (steps, 512, width), (steps, 8, 128)
    space = pltpu.HBM if stored else VMEM
    scratch = [
        pltpu.VMEM(shape, F8),
        pltpu.VMEM(small, jnp.float32),
        pltpu.SemaphoreType.DMA((steps + 1, 4)),
    ]
    return pl.pallas_call(
        stored_theory_kernel if stored else theory_kernel,
        out_shape=(space(shape, F8), space(small, jnp.float32)),
        in_specs=[pl.BlockSpec(memory_space=VMEM)],
        out_specs=(pl.BlockSpec(memory_space=space),) * 2,
        scratch_shapes=scratch if stored else [],
        compiler_params=pltpu.CompilerParams(vmem_limit_bytes=(8 if stored else 4) << 20),
        cost_estimate=pl.CostEstimate(
            flops=2_000_000_000, bytes_accessed=6_400_000, transcendentals=0
        ),
        name="theory",
    )(flat)


def score_kernel(
    counts_ref,
    stored_hbm,
    stored_largest_hbm,
    theory_ref,
    largest_ref,
    flat0_ref,
    flat1_ref,
    flat2_ref,
    flat3_ref,
    own_ref,
    other_ref,
    out_ref,
    held,
    held_largest,
    built2,
    built3,
    halves,
    stats_ref,
    exact,
    tables_ref,
    sems,
):
    steps, width = theory_ref.shape[0], theory_ref.shape[2]
    flats = (flat0_ref, flat1_ref, flat2_ref, flat3_ref)

    def copy_of(step):
        return pltpu.make_async_copy(stored_hbm.at[step], held.at[step], sems.at[step])

    small = pltpu.make_async_copy(stored_largest_hbm, held_largest, sems.at[steps])
    small.start()
    for step in range(steps):
        copy_of(step).start()
    y = lax.axis_index("spec") // 2
    core = lax.axis_index("spec") % 2
    mass = lax.axis_index("mass")
    rows = own_ref.shape[0]
    local = (iota((512, 1), 0) % 4) * 128 + iota((512, 1), 0) // 4
    entry = iota((32 * steps, rows), 0)
    source = (entry % 32 // 2) * SLOTS + entry // 32 * 2 + entry % 2
    pick = jnp.where(iota((32 * steps, rows), 1) == source, 1.0, 0.0).astype(jnp.bfloat16)
    for half, ref in enumerate((own_ref, other_ref)):
        values = jnp.dot(pick, ref[...], preferred_element_type=jnp.float32)
        upper = values.astype(F8)
        lower = ((values - upper.astype(jnp.float32)) * 32.0).astype(F8)
        for step in range(steps):
            rows_now = slice(step * 32, step * 32 + 32)
            at = half * 32
            halves[step, at : at + 32, :] = upper[rows_now]
            halves[step, 64 + at : 96 + at, :] = lower[rows_now]
    small.wait()

    def reduced(scores, limit):
        valid = local < limit
        best = jnp.max(jnp.where(valid, scores, -1e30), axis=0, keepdims=True)
        scores = jnp.where(valid, scores, 0.0)
        return (
            best,
            jnp.sum(scores, axis=0, keepdims=True),
            jnp.sum(scores * scores, axis=0, keepdims=True),
        )

    def base_of(turn):
        return (lax.rem(y + turn, 4) * 2 + core) * 512

    def keep(step, found):
        stats_ref[step, 0:1, :] = functools.reduce(jnp.maximum, [item[0] for item in found])
        for row in (1, 2):
            stats_ref[step, row : row + 1, :] = functools.reduce(
                jnp.add, [item[row] for item in found]
            )

    def window(step, largest):
        live = counts_ref[mass * steps + step]
        largest = jnp.maximum(largest, theory_of(flat2_ref[step].astype(jnp.int32), built2))
        largest = jnp.maximum(largest, theory_of(flat3_ref[step].astype(jnp.int32), built3))
        largest = jnp.maximum(largest, jnp.maximum(held_largest[step], largest_ref[step]))
        copy_of(step).wait()
        found = []
        for turn, theory in enumerate((held.at[step], theory_ref.at[step], built2, built3)):
            scores = lax.dot_general(
                theory[...],
                halves[step],
                (((1,), (1,)), ((), ())),
                preferred_element_type=jnp.float32,
            )
            scores = scores + pltpu.roll(scores, 64, 1) * (1.0 / 32.0)
            found.append(reduced(scores, live - base_of(turn)))
        keep(step, found)
        return largest

    def exact_window(step, carry):
        live = counts_ref[mass * steps + step]
        for turn in range(4):
            tables_ref[turn] = flats[turn][step].astype(jnp.int32)
        own_entry = iota((64, rows), 0)
        mine = (own_entry % 32 // 2) * SLOTS + step * 2 + own_entry % 2
        mine = iota((64, rows), 1) == mine
        values = sum(
            jnp.dot(
                jnp.where(mine & (own_entry // 32 == half), 1.0, 0.0).astype(jnp.bfloat16),
                ref[...],
                preferred_element_type=jnp.float32,
            )
            for half, ref in enumerate((own_ref, other_ref))
        ).astype(jnp.bfloat16)
        values = jnp.concatenate([values, jnp.zeros_like(values)], axis=0)

        def piece(turn, found):
            theory_of(tables_ref[turn], exact)
            scores = lax.dot_general(
                exact[...],
                values,
                (((1,), (1,)), ((), ())),
                preferred_element_type=jnp.float32,
            )
            more = reduced(scores, live - base_of(turn))
            return (
                jnp.maximum(found[0], more[0]),
                found[1] + more[1],
                found[2] + more[2],
            )

        zeros = jnp.zeros((1, 128), jnp.float32)
        keep(step, [lax.fori_loop(0, 4, piece, (zeros - 1e30, zeros, zeros))])
        return carry

    stats_ref[...] = jnp.zeros_like(stats_ref)
    largest = lax.fori_loop(0, steps, window, jnp.zeros((8, 128), jnp.float32))

    @pl.when(jnp.max(largest) > 16.0)
    def _():
        lax.fori_loop(0, steps, exact_window, 0)

    part = iota((8, 128), 1) // 32
    place = iota((1, 128), 1) % 32 // 4
    tiles = []
    for half in range(2):
        tile = jnp.zeros((8, 128), jnp.float32)
        for step in range(steps):
            moved = pltpu.roll(stats_ref[step], (step * 32 - half * 32) % 128, 1)
            tile = jnp.where(part == step, moved, tile)
        tiles.append(tile)
    first = jnp.where(core == 0, tiles[0], tiles[1])
    second = jnp.where(core == 0, tiles[1], tiles[0])
    peers = out_ref.shape[0] // 2
    for half, tile in enumerate((first, second)):
        for peer in range(peers):
            row = jnp.zeros((1, 128), jnp.float32)
            for stat in range(3):
                moved = pltpu.roll(tile, (4 * stat - 2 * peer) % 128, 1)[stat : stat + 1]
                row = jnp.where(place == stat, moved, row)
            at = half * peers + peer
            out_ref[at : at + 1, :] = row


def finish_kernel(where_hbm, stats_hbm, best_ref, z_ref, where_ref, stats_ref, sems):
    copies = [
        pltpu.make_async_copy(stats_hbm, stats_ref, sems.at[0]),
        pltpu.make_async_copy(where_hbm, where_ref, sems.at[1]),
    ]
    for copy in copies:
        copy.start()
    for copy in copies:
        copy.wait()
    rows = best_ref.shape[1]
    peers = stats_ref.shape[0] // 2
    lane = where_ref[0:1, :].astype(jnp.int32)
    shard = where_ref[1:2, :].astype(jnp.int32)
    live = where_ref[2:3, :]
    unscale = 1.0 / (where_ref[3:4, :] * 32.0)
    mine = iota((peers, 128), 0) == shard
    picked = []
    for stat in range(3):
        index = jnp.broadcast_to(lane + 4 * stat, (peers, 128))
        for half in range(2):
            found = jnp.take_along_axis(
                stats_ref[half * peers : (half + 1) * peers, :], index, axis=1
            )
            picked.append(jnp.sum(jnp.where(mine, found, 0.0), axis=0, keepdims=True))
    best = jnp.maximum(picked[0], picked[1]) * unscale
    total = (picked[2] + picked[3]) * unscale
    square = (picked[4] + picked[5]) * unscale * unscale
    mean = total / live
    spread = square / live - mean * mean
    z = (best - mean) / jnp.sqrt(spread + EPS)
    best_ref[0:1, :] = best[:, :rows]
    best_ref[1:2, :] = best[:, rows : 2 * rows]
    z_ref[0:1, :] = z[:, :rows]
    z_ref[1:2, :] = z[:, rows : 2 * rows]


def per_device(spectra, routes, pep_bins, counts):
    rows, width = spectra.shape
    mass_count = lax.axis_size("mass")
    spec_count = lax.axis_size("spec")
    steps = pep_bins.shape[0]
    routes_t = routes.T
    vmem = pl.BlockSpec(memory_space=VMEM)
    smem = pl.BlockSpec(memory_space=SMEM)
    hbm = pl.BlockSpec(memory_space=pltpu.HBM)
    outgoing, flat, where = pl.pallas_call(
        prepare_kernel,
        out_shape=(
            pltpu.HBM((mass_count * SLOTS, width), jnp.bfloat16),
            jax.ShapeDtypeStruct((steps, 128, 128), jnp.int16),
            pltpu.HBM((8, 128), jnp.float32),
        ),
        in_specs=[hbm] * 4,
        out_specs=(hbm, vmem, hbm),
        scratch_shapes=[
            pltpu.VMEM((mass_count * SLOTS, width), jnp.bfloat16),
            pltpu.VMEM((8, 128), jnp.float32),
            pltpu.SMEM(counts.shape, counts.dtype),
            pltpu.VMEM((rows, width), spectra.dtype),
            pltpu.VMEM(routes_t.shape, routes_t.dtype),
            pltpu.VMEM(pep_bins.shape, pep_bins.dtype),
            pltpu.VMEM((rows, width + 2 * PAD), jnp.bfloat16),
            pltpu.SemaphoreType.DMA((5 + width // 256,)),
        ],
        compiler_params=pltpu.CompilerParams(vmem_limit_bytes=8 << 20),
        name="prepare",
    )(
        *[
            pltpu.with_memory_space_constraint(item, pltpu.HBM)
            for item in (spectra, routes_t, pep_bins, counts)
        ]
    )
    flats = [flat] + [
        lax.ppermute(
            flat, "spec", [((i + 2 * turn) % spec_count, i) for i in range(spec_count)]
        )
        for turn in range(1, 4)
    ]
    own = lax.all_to_all(outgoing, "mass", split_axis=0, concat_axis=0, tiled=True)
    first, first_largest = build_theory(flats[0], width, True)
    own, first, flats = lax.optimization_barrier((own, first, flats))
    other = lax.ppermute(own, "spec", [(i, i ^ 1) for i in range(spec_count)])
    second, second_largest = build_theory(flats[1], width, False)
    stats = pl.pallas_call(
        score_kernel,
        out_shape=jax.ShapeDtypeStruct((2 * mass_count, 128), jnp.float32),
        in_specs=[smem, hbm, hbm] + [vmem] * 8,
        out_specs=vmem,
        scratch_shapes=[
            pltpu.VMEM((steps, 512, width), F8),
            pltpu.VMEM((steps, 8, 128), jnp.float32),
            pltpu.VMEM((512, width), F8),
            pltpu.VMEM((512, width), F8),
            pltpu.VMEM((steps, 128, width), F8),
            pltpu.VMEM((steps, 8, 128), jnp.float32),
            pltpu.VMEM((512, width), jnp.bfloat16),
            pltpu.VMEM((4, 128, 128), jnp.int32),
            pltpu.SemaphoreType.DMA((steps + 1,)),
        ],
        compiler_params=pltpu.CompilerParams(vmem_limit_bytes=24 << 20),
        name="score",
    )(
        counts,
        pltpu.with_memory_space_constraint(first, pltpu.HBM),
        pltpu.with_memory_space_constraint(first_largest, pltpu.HBM),
        second,
        second_largest,
        *flats,
        own,
        other,
    )
    groups = [
        [(y * 2 + core) * mass_count + m for core in range(2) for m in range(mass_count)]
        for y in range(spec_count // 2)
    ]
    back = lax.all_to_all(
        stats,
        ("spec", "mass"),
        split_axis=0,
        concat_axis=0,
        tiled=True,
        axis_index_groups=groups,
    )
    best, z = pl.pallas_call(
        finish_kernel,
        out_shape=(jax.ShapeDtypeStruct((2, rows), jnp.float32),) * 2,
        in_specs=[hbm] * 2,
        out_specs=(vmem, vmem),
        scratch_shapes=[
            pltpu.VMEM((8, 128), jnp.float32),
            pltpu.VMEM(back.shape, jnp.float32),
            pltpu.SemaphoreType.DMA((2,)),
        ],
        name="finish",
    )(*[pltpu.with_memory_space_constraint(item, pltpu.HBM) for item in (where, back)])
    return best.T, z.T


def solution(mesh):
    return jax.shard_map(
        per_device,
        mesh=mesh,
        in_specs=(
            P(("spec", "mass"), None),
            P(("spec", "mass"), None),
            P("mass", None, "spec"),
            P(),
        ),
        out_specs=(P(("spec", "mass"), None), P(("spec", "mass"), None)),
        check_vma=False,
    )
```

```python
import functools

import jax
import jax.numpy as jnp
from jax import lax
from jax.experimental import pallas as pl
from jax.experimental.pallas import tpu as pltpu
from jax.sharding import PartitionSpec as P

LAG = 75
EPS = 1e-06
PAD = 128
SLOTS = 8
LOW = 128
HIGH = 16
F8 = jnp.float8_e4m3fn
VMEM = pltpu.VMEM
SMEM = pltpu.SMEM


def iota(shape, axis):
    return lax.broadcasted_iota(jnp.int32, shape, axis)


def prepare_kernel(
    spectra_hbm,
    routes_hbm,
    pep_hbm,
    counts_hbm,
    out_hbm,
    flat_ref,
    where_hbm,
    out_ref,
    where_ref,
    counts_ref,
    spectra_ref,
    routes_ref,
    pep_ref,
    padded,
    sems,
):
    copies = [
        pltpu.make_async_copy(spectra_hbm, spectra_ref, sems.at[0]),
        pltpu.make_async_copy(routes_hbm, routes_ref, sems.at[1]),
        pltpu.make_async_copy(pep_hbm, pep_ref, sems.at[2]),
        pltpu.make_async_copy(counts_hbm, counts_ref, sems.at[3]),
    ]
    for copy in copies:
        copy.start()
    rows, width = spectra_ref.shape
    block = 256
    gap = jnp.abs(iota((block + 2 * PAD, block), 0) - PAD - iota((block + 2 * PAD, block), 1))
    band = jnp.where((gap > 0) & (gap <= LAG), 1.0, 0.0).astype(jnp.bfloat16)
    copies[0].wait()
    rooted = jnp.sqrt(spectra_ref[...].astype(jnp.float32)).astype(jnp.bfloat16)
    padded[:, :PAD] = jnp.zeros((rows, PAD), jnp.bfloat16)
    padded[:, PAD + width :] = jnp.zeros((rows, PAD), jnp.bfloat16)
    padded[:, PAD : PAD + width] = rooted
    peak = jnp.max(rooted.astype(jnp.float32), axis=1, keepdims=True)
    scale = jnp.ones((rows, 1), jnp.float32)
    for power in (16, 8, 4, 2, 1):
        larger = scale * 2.0**power
        scale = jnp.where(peak * larger <= 256.0, larger, scale)
    copies[1].wait()
    place = iota((out_ref.shape[0], rows), 0)
    inner = place % SLOTS
    window = (place // SLOTS) * 3 + inner // 2
    named = (routes_ref[0:1, :] == window) | (routes_ref[1:2, :] == window)
    named = named & (inner < 6)
    before = jnp.where(iota((rows, rows), 0) < iota((rows, rows), 1), 1.0, 0.0)
    earlier = jnp.dot(
        jnp.where(named, 1.0, 0.0).astype(jnp.bfloat16),
        before.astype(jnp.bfloat16),
        preferred_element_type=jnp.float32,
    )
    taken = named & (earlier == (inner % 2).astype(jnp.float32))
    routing = jnp.where(taken, 1.0, 0.0).astype(jnp.bfloat16)
    blocks = [padded[:, start : start + block + 2 * PAD] for start in range(0, width, block)]
    background = jnp.dot(
        jnp.concatenate(blocks, axis=0), band, preferred_element_type=jnp.float32
    )
    leaving = []
    for start in range(0, width, block):
        at = start // block * rows
        values = rooted[:, start : start + block].astype(jnp.float32)
        prepared = values - background[at : at + rows] / (2.0 * LAG)
        prepared = prepared.astype(jnp.bfloat16)
        prepared = (prepared.astype(jnp.float32) * scale).astype(jnp.bfloat16)
        out_ref[:, start : start + block] = jnp.dot(
            routing, prepared, preferred_element_type=jnp.float32
        ).astype(jnp.bfloat16)
        columns = pl.ds(start, block)
        leaving.append(
            pltpu.make_async_copy(
                out_ref.at[:, columns], out_hbm.at[:, columns], sems.at[5 + start // block]
            )
        )
        leaving[-1].start()
    copies[3].wait()
    windows = counts_ref.shape[0]
    named_by = routes_ref[...]
    live = jnp.zeros(named_by.shape, jnp.int32)
    for index in range(windows):
        live = jnp.where(named_by == index, counts_ref[index], live)
    where_ref[...] = jnp.zeros_like(where_ref)
    diagonal = iota((rows, rows), 0) == iota((rows, rows), 1)
    turned_scale = jnp.sum(jnp.where(diagonal, scale, 0.0), axis=0, keepdims=True)
    for pick in range(2):
        here = routes_ref[pick : pick + 1, :]
        mine = taken & (window == here)
        found = jnp.sum(jnp.where(mine, place, 0), axis=0, keepdims=True)
        lanes = slice(pick * rows, (pick + 1) * rows)
        inside = found % SLOTS
        where_ref[0:1, lanes] = ((inside // 2) * 32 + inside % 2).astype(jnp.float32)
        where_ref[1:2, lanes] = (found // SLOTS).astype(jnp.float32)
        where_ref[2:3, lanes] = live[pick : pick + 1].astype(jnp.float32)
        where_ref[3:4, lanes] = turned_scale
    leaving.append(pltpu.make_async_copy(where_ref, where_hbm, sems.at[4]))
    leaving[-1].start()
    copies[2].wait()
    for step in range(pep_ref.shape[0]):
        table = pep_ref[step]
        parts = [table[:, part * 128 : part * 128 + 128] for part in range(4)]
        flat_ref[step] = jnp.concatenate(parts, axis=0).T.astype(jnp.int16)
    for copy in leaving:
        copy.wait()


def theory_of(bins, theory_ref, finished=None):
    width = bins.shape[1]
    high_place = iota((HIGH * 8, 2 * width), 0).astype(jnp.float32).astype(jnp.bfloat16)
    low_place = iota((LOW, 2 * width), 0).astype(jnp.float32).astype(jnp.bfloat16)
    one = jnp.ones((), F8)
    zero = jnp.zeros((), F8)
    member = iota((128, 128), 1) // 32 + 4 * (iota((128, 128), 0) % 2)
    low = (bins & (LOW - 1)).astype(jnp.float32).astype(jnp.bfloat16)
    high = ((bins >> 7) * 8 + member).astype(jnp.float32).astype(jnp.bfloat16)
    largest = jnp.zeros((8, 128), jnp.float32)
    for quad in range(16):
        parts = []
        for item in range(4):
            row = 8 * quad + 2 * item
            high_row = jnp.concatenate([high[row : row + 1], high[row + 1 : row + 2]], axis=1)
            low_row = jnp.concatenate([low[row : row + 1], low[row + 1 : row + 2]], axis=1)
            parts.append(
                lax.dot_general(
                    jnp.where(high_place == high_row, one, zero),
                    jnp.where(low_place == low_row, one, zero),
                    (((1,), (1,)), ((), ())),
                    preferred_element_type=jnp.float32,
                )
            )
        for part in range(HIGH):
            pieces = [item[part * 8 : part * 8 + 8] for item in parts]
            theory_ref[quad * 32 : quad * 32 + 32, part * LOW : (part + 1) * LOW] = (
                jnp.concatenate(pieces, axis=0).astype(theory_ref.dtype)
            )
            more = jnp.maximum(
                jnp.maximum(pieces[0], pieces[1]), jnp.maximum(pieces[2], pieces[3])
            )
            largest = jnp.maximum(largest, more)
        if finished is not None and quad % 4 == 3:
            finished(quad // 4)
    return largest


def theory_kernel(flat_ref, theory_ref, largest_ref):
    def window(step, carry):
        largest_ref[step] = theory_of(flat_ref[step].astype(jnp.int32), theory_ref.at[step])
        return carry

    for step in range(flat_ref.shape[0]):
        window(step, 0)


def stored_theory_kernel(flat_ref, theory_hbm, largest_hbm, held, largest, sems):
    steps = flat_ref.shape[0]

    def copy_of(step, quarter):
        rows = pl.ds(quarter * 128, 128)
        return pltpu.make_async_copy(
            held.at[step, rows], theory_hbm.at[step, rows], sems.at[step, quarter]
        )

    def window(step, carry):
        largest[step] = theory_of(
            flat_ref[step].astype(jnp.int32),
            held.at[step],
            lambda quarter: copy_of(step, quarter).start(),
        )
        return carry

    for step in range(steps):
        window(step, 0)
    last = pltpu.make_async_copy(largest, largest_hbm, sems.at[steps, 0])
    last.start()
    for step in range(steps):
        for quarter in range(4):
            copy_of(step, quarter).wait()
    last.wait()


def build_theory(flat, width, stored):
    steps = flat.shape[0]
    shape, small = (steps, 512, width), (steps, 8, 128)
    space = pltpu.HBM if stored else VMEM
    scratch = [
        pltpu.VMEM(shape, F8),
        pltpu.VMEM(small, jnp.float32),
        pltpu.SemaphoreType.DMA((steps + 1, 4)),
    ]
    return pl.pallas_call(
        stored_theory_kernel if stored else theory_kernel,
        out_shape=(space(shape, F8), space(small, jnp.float32)),
        in_specs=[pl.BlockSpec(memory_space=VMEM)],
        out_specs=(pl.BlockSpec(memory_space=space),) * 2,
        scratch_shapes=scratch if stored else [],
        compiler_params=pltpu.CompilerParams(vmem_limit_bytes=(8 if stored else 4) << 20),
        cost_estimate=pl.CostEstimate(
            flops=2_000_000_000, bytes_accessed=6_400_000, transcendentals=0
        ),
        name="theory",
    )(flat)


def score_kernel(
    counts_ref,
    stored_hbm,
    stored_largest_hbm,
    theory_ref,
    largest_ref,
    flat0_ref,
    flat1_ref,
    flat2_ref,
    flat3_ref,
    own_ref,
    other_ref,
    out_ref,
    held,
    held_largest,
    built2,
    built3,
    halves,
    stats_ref,
    exact,
    tables_ref,
    sems,
):
    steps, width = theory_ref.shape[0], theory_ref.shape[2]
    flats = (flat0_ref, flat1_ref, flat2_ref, flat3_ref)

    def copy_of(step):
        return pltpu.make_async_copy(stored_hbm.at[step], held.at[step], sems.at[step])

    small = pltpu.make_async_copy(stored_largest_hbm, held_largest, sems.at[steps])
    small.start()
    for step in range(steps):
        copy_of(step).start()
    y = lax.axis_index("spec") // 2
    core = lax.axis_index("spec") % 2
    mass = lax.axis_index("mass")
    rows = own_ref.shape[0]
    local = (iota((512, 1), 0) % 4) * 128 + iota((512, 1), 0) // 4
    entry = iota((32 * steps, rows), 0)
    source = (entry % 32 // 2) * SLOTS + entry // 32 * 2 + entry % 2
    pick = jnp.where(iota((32 * steps, rows), 1) == source, 1.0, 0.0).astype(jnp.bfloat16)
    for half, ref in enumerate((own_ref, other_ref)):
        values = jnp.dot(pick, ref[...], preferred_element_type=jnp.float32)
        upper = values.astype(F8)
        lower = ((values - upper.astype(jnp.float32)) * 32.0).astype(F8)
        for step in range(steps):
            rows_now = slice(step * 32, step * 32 + 32)
            at = half * 32
            halves[step, at : at + 32, :] = upper[rows_now]
            halves[step, 64 + at : 96 + at, :] = lower[rows_now]
    small.wait()

    def reduced(scores, limit):
        valid = local < limit
        best = jnp.max(jnp.where(valid, scores, -1e30), axis=0, keepdims=True)
        scores = jnp.where(valid, scores, 0.0)
        return (
            best,
            jnp.sum(scores, axis=0, keepdims=True),
            jnp.sum(scores * scores, axis=0, keepdims=True),
        )

    def base_of(turn):
        return (lax.rem(y + turn, 4) * 2 + core) * 512

    def keep(step, found):
        stats_ref[step, 0:1, :] = functools.reduce(jnp.maximum, [item[0] for item in found])
        for row in (1, 2):
            stats_ref[step, row : row + 1, :] = functools.reduce(
                jnp.add, [item[row] for item in found]
            )

    def window(step, largest):
        live = counts_ref[mass * steps + step]
        largest = jnp.maximum(largest, theory_of(flat2_ref[step].astype(jnp.int32), built2))
        largest = jnp.maximum(largest, theory_of(flat3_ref[step].astype(jnp.int32), built3))
        largest = jnp.maximum(largest, jnp.maximum(held_largest[step], largest_ref[step]))
        copy_of(step).wait()
        found = []
        for turn, theory in enumerate((held.at[step], theory_ref.at[step], built2, built3)):
            scores = lax.dot_general(
                theory[...],
                halves[step],
                (((1,), (1,)), ((), ())),
                preferred_element_type=jnp.float32,
            )
            scores = scores + pltpu.roll(scores, 64, 1) * (1.0 / 32.0)
            found.append(reduced(scores, live - base_of(turn)))
        keep(step, found)
        return largest

    def exact_window(step, carry):
        live = counts_ref[mass * steps + step]
        for turn in range(4):
            tables_ref[turn] = flats[turn][step].astype(jnp.int32)
        own_entry = iota((64, rows), 0)
        mine = (own_entry % 32 // 2) * SLOTS + step * 2 + own_entry % 2
        mine = iota((64, rows), 1) == mine
        values = sum(
            jnp.dot(
                jnp.where(mine & (own_entry // 32 == half), 1.0, 0.0).astype(jnp.bfloat16),
                ref[...],
                preferred_element_type=jnp.float32,
            )
            for half, ref in enumerate((own_ref, other_ref))
        ).astype(jnp.bfloat16)
        values = jnp.concatenate([values, jnp.zeros_like(values)], axis=0)

        def piece(turn, found):
            theory_of(tables_ref[turn], exact)
            scores = lax.dot_general(
                exact[...],
                values,
                (((1,), (1,)), ((), ())),
                preferred_element_type=jnp.float32,
            )
            more = reduced(scores, live - base_of(turn))
            return (
                jnp.maximum(found[0], more[0]),
                found[1] + more[1],
                found[2] + more[2],
            )

        zeros = jnp.zeros((1, 128), jnp.float32)
        keep(step, [lax.fori_loop(0, 4, piece, (zeros - 1e30, zeros, zeros))])
        return carry

    stats_ref[...] = jnp.zeros_like(stats_ref)
    largest = lax.fori_loop(0, steps, window, jnp.zeros((8, 128), jnp.float32))

    @pl.when(jnp.max(largest) > 16.0)
    def _():
        lax.fori_loop(0, steps, exact_window, 0)

    part = iota((8, 128), 1) // 32
    place = iota((1, 128), 1) % 32 // 4
    tiles = []
    for half in range(2):
        tile = jnp.zeros((8, 128), jnp.float32)
        for step in range(steps):
            moved = pltpu.roll(stats_ref[step], (step * 32 - half * 32) % 128, 1)
            tile = jnp.where(part == step, moved, tile)
        tiles.append(tile)
    first = jnp.where(core == 0, tiles[0], tiles[1])
    second = jnp.where(core == 0, tiles[1], tiles[0])
    peers = out_ref.shape[0] // 2
    for half, tile in enumerate((first, second)):
        for peer in range(peers):
            row = jnp.zeros((1, 128), jnp.float32)
            for stat in range(3):
                moved = pltpu.roll(tile, (4 * stat - 2 * peer) % 128, 1)[stat : stat + 1]
                row = jnp.where(place == stat, moved, row)
            at = half * peers + peer
            out_ref[at : at + 1, :] = row


def finish_kernel(where_hbm, stats_hbm, best_ref, z_ref, where_ref, stats_ref, sems):
    copies = [
        pltpu.make_async_copy(stats_hbm, stats_ref, sems.at[0]),
        pltpu.make_async_copy(where_hbm, where_ref, sems.at[1]),
    ]
    for copy in copies:
        copy.start()
    for copy in copies:
        copy.wait()
    rows = best_ref.shape[1]
    peers = stats_ref.shape[0] // 2
    lane = where_ref[0:1, :].astype(jnp.int32)
    shard = where_ref[1:2, :].astype(jnp.int32)
    live = where_ref[2:3, :]
    unscale = 1.0 / (where_ref[3:4, :] * 32.0)
    mine = iota((peers, 128), 0) == shard
    picked = []
    for stat in range(3):
        index = jnp.broadcast_to(lane + 4 * stat, (peers, 128))
        for half in range(2):
            found = jnp.take_along_axis(
                stats_ref[half * peers : (half + 1) * peers, :], index, axis=1
            )
            picked.append(jnp.sum(jnp.where(mine, found, 0.0), axis=0, keepdims=True))
    best = jnp.maximum(picked[0], picked[1]) * unscale
    total = (picked[2] + picked[3]) * unscale
    square = (picked[4] + picked[5]) * unscale * unscale
    mean = total / live
    spread = square / live - mean * mean
    z = (best - mean) / jnp.sqrt(spread + EPS)
    best_ref[0:1, :] = best[:, :rows]
    best_ref[1:2, :] = best[:, rows : 2 * rows]
    z_ref[0:1, :] = z[:, :rows]
    z_ref[1:2, :] = z[:, rows : 2 * rows]


def per_device(spectra, routes, pep_bins, counts):
    rows, width = spectra.shape
    mass_count = lax.axis_size("mass")
    spec_count = lax.axis_size("spec")
    steps = pep_bins.shape[0]
    routes_t = routes.T
    vmem = pl.BlockSpec(memory_space=VMEM)
    smem = pl.BlockSpec(memory_space=SMEM)
    hbm = pl.BlockSpec(memory_space=pltpu.HBM)
    outgoing, flat, where = pl.pallas_call(
        prepare_kernel,
        out_shape=(
            pltpu.HBM((mass_count * SLOTS, width), jnp.bfloat16),
            jax.ShapeDtypeStruct((steps, 128, 128), jnp.int16),
            pltpu.HBM((8, 128), jnp.float32),
        ),
        in_specs=[hbm] * 4,
        out_specs=(hbm, vmem, hbm),
        scratch_shapes=[
            pltpu.VMEM((mass_count * SLOTS, width), jnp.bfloat16),
            pltpu.VMEM((8, 128), jnp.float32),
            pltpu.SMEM(counts.shape, counts.dtype),
            pltpu.VMEM((rows, width), spectra.dtype),
            pltpu.VMEM(routes_t.shape, routes_t.dtype),
            pltpu.VMEM(pep_bins.shape, pep_bins.dtype),
            pltpu.VMEM((rows, width + 2 * PAD), jnp.bfloat16),
            pltpu.SemaphoreType.DMA((5 + width // 256,)),
        ],
        compiler_params=pltpu.CompilerParams(vmem_limit_bytes=8 << 20),
        name="prepare",
    )(
        *[
            pltpu.with_memory_space_constraint(item, pltpu.HBM)
            for item in (spectra, routes_t, pep_bins, counts)
        ]
    )
    flats = [flat] + [
        lax.ppermute(
            flat, "spec", [((i + 2 * turn) % spec_count, i) for i in range(spec_count)]
        )
        for turn in range(1, 4)
    ]
    own = lax.all_to_all(outgoing, "mass", split_axis=0, concat_axis=0, tiled=True)
    first, first_largest = build_theory(flats[0], width, True)
    own, first, flats = lax.optimization_barrier((own, first, flats))
    other = lax.ppermute(own, "spec", [(i, i ^ 1) for i in range(spec_count)])
    second, second_largest = build_theory(flats[1], width, False)
    stats = pl.pallas_call(
        score_kernel,
        out_shape=jax.ShapeDtypeStruct((2 * mass_count, 128), jnp.float32),
        in_specs=[smem, hbm, hbm] + [vmem] * 8,
        out_specs=vmem,
        scratch_shapes=[
            pltpu.VMEM((steps, 512, width), F8),
            pltpu.VMEM((steps, 8, 128), jnp.float32),
            pltpu.VMEM((512, width), F8),
            pltpu.VMEM((512, width), F8),
            pltpu.VMEM((steps, 128, width), F8),
            pltpu.VMEM((steps, 8, 128), jnp.float32),
            pltpu.VMEM((512, width), jnp.bfloat16),
            pltpu.VMEM((4, 128, 128), jnp.int32),
            pltpu.SemaphoreType.DMA((steps + 1,)),
        ],
        compiler_params=pltpu.CompilerParams(vmem_limit_bytes=24 << 20),
        name="score",
    )(
        counts,
        pltpu.with_memory_space_constraint(first, pltpu.HBM),
        pltpu.with_memory_space_constraint(first_largest, pltpu.HBM),
        second,
        second_largest,
        *flats,
        own,
        other,
    )
    groups = [
        [(y * 2 + core) * mass_count + m for core in range(2) for m in range(mass_count)]
        for y in range(spec_count // 2)
    ]
    back = lax.all_to_all(
        stats,
        ("spec", "mass"),
        split_axis=0,
        concat_axis=0,
        tiled=True,
        axis_index_groups=groups,
    )
    best, z = pl.pallas_call(
        finish_kernel,
        out_shape=(jax.ShapeDtypeStruct((2, rows), jnp.float32),) * 2,
        in_specs=[hbm] * 2,
        out_specs=(vmem, vmem),
        scratch_shapes=[
            pltpu.VMEM((8, 128), jnp.float32),
            pltpu.VMEM(back.shape, jnp.float32),
            pltpu.SemaphoreType.DMA((2,)),
        ],
        name="finish",
    )(*[pltpu.with_memory_space_constraint(item, pltpu.HBM) for item in (where, back)])
    return best.T, z.T


def solution(mesh):
    return jax.shard_map(
        per_device,
        mesh=mesh,
        in_specs=(
            P(("spec", "mass"), None),
            P(("spec", "mass"), None),
            P("mass", None, "spec"),
            P(),
        ),
        out_specs=(P(("spec", "mass"), None), P(("spec", "mass"), None)),
        check_vma=False,
    )
```
